32 devices in a mesh: groups: 2 (over y), ctx: 4 (over z), dp: 4 (over x, core).
Axes of the slice: x: 2, y: 2, z: 4, core: 2. Of those that a mesh axis runs over, the one named last changes fastest.
Arguments:
- tokens: int32 [8, 1024, 128], P(('groups', 'dp'), 'ctx'), parts along dimension 0, may hold values from 0 to 3
- targets: int32 [8, 1024, 896], P(('groups', 'dp'), 'ctx'), parts along dimension 0, may hold values from 0 to 3
- stem_half: bfloat16 [1024, 384], P('groups'), parts along dimension 0, may hold values from -0.5 to 0.5
- conv_half: bfloat16 [10, 768, 256], P('groups'), parts along dimension 0, may hold values from -0.09375 to 0.09375
- point_half: bfloat16 [1024, 384], P('groups'), parts along dimension 0, may hold values from -0.25 to 0.25
- head_half: bfloat16 [768, 896], P('groups'), parts along dimension 0, may hold values from -0.21875 to 0.21875
Outputs:
- grad_stem: float32 [1024, 384], P(('groups', 'ctx', 'dp')), parts along dimension 0
- grad_conv: float32 [7680, 256], P(('groups', 'ctx', 'dp')), parts along dimension 0
- grad_point: float32 [1024, 384], P(('groups', 'ctx', 'dp')), parts along dimension 0
- grad_head: float32 [1792, 384], P(('groups', 'ctx', 'dp')), parts along dimension 0
The draws below stay inside these ranges and needn't reach their ends.
There are 2 independent parts, one for each index of `groups`. The reference program is written for one: setup_inputs(seed, part) draws one part's arguments, and reference() takes and returns one part's arrays. A program takes and returns all parts, laid end to end along the dimension named above; each array names one. Nothing has to cross between parts.
All inputs are finite; a program needn't handle non-finite values.
Results may differ from the reference program's by a relative error of at most 0.00095.
Values may be sent and summed in bfloat16 or wider, within the bound.
A program may use at most 64 MiB of HBM per device.

```python
import math
import jax
import jax.numpy as jnp
from jax import lax

C = 768
H = 512
TRACKS = 896
KW = 5
BIN = 128
DILATION_STEP = 128
LENGTH = 1024
SEQS = 4


def set_ends(array, own_key, smallest, largest):
    longest = array.shape.index(max(array.shape))
    spots = []
    for shift in (0, 1):
        where = [jax.random.randint(jax.random.fold_in(own_key, axis), (), 0, length) for axis, length in enumerate(array.shape)]
        where[longest] = (where[longest] + shift) % array.shape[longest]
        spots.append(tuple(where))
    return array.at[spots[0]].set(smallest).at[spots[1]].set(largest)


def scatter_about(rng, extent, deviation, bound, kind=jnp.bfloat16):
    return jnp.clip(deviation * jax.random.normal(rng, extent, jnp.float32), -bound, bound).astype(kind)


def setup_inputs(seed: int = 0, part: int = 0) -> dict:
    keys = jax.random.split(jax.random.key(seed), 7)
    part_splits = jax.random.split(jax.random.fold_in(keys[6], part), 7)
    return {
        "tokens": set_ends(jax.random.randint(part_splits[0], (SEQS, LENGTH, BIN), 0, 4), jax.random.fold_in(part_splits[0], 1), 0, 3).astype(jnp.int32),
        "targets": set_ends(jax.random.randint(part_splits[1], (SEQS, LENGTH, TRACKS), 0, 4), jax.random.fold_in(part_splits[1], 1), 0, 3).astype(jnp.int32),
        "stem_half": scatter_about(part_splits[2], (4 * BIN, C // 2), BIN ** -0.5, 0.5),
        "conv_half": scatter_about(part_splits[3], (KW, C, H // 2), (KW * C) ** -0.5, 0.09375),
        "point_half": scatter_about(part_splits[4], (H, C // 2), H ** -0.5, 0.25),
        "head_half": scatter_about(part_splits[5], (C // 2, TRACKS), C ** -0.5, 0.21875),
    }


def expand_weights(stem_half, conv_half, point_half, head_half):
    stem_full = jnp.concatenate([stem_half, stem_half[::-1, ::-1]], axis=1)
    conv_full = jnp.concatenate([conv_half, conv_half[::-1, ::-1, ::-1]], axis=2)
    point_full = jnp.concatenate([point_half, point_half[::-1, ::-1]], axis=1)
    head_full = jnp.concatenate([head_half, head_half[::-1, :]], axis=0)
    return (stem_full, conv_full, point_full, head_full)

def gelu_slope(values):
    normal_cdf = 0.5 * (1.0 + lax.erf(values * (1.0 / math.sqrt(2.0))))
    normal_pdf = jnp.exp(-0.5 * values * values) * (1.0 / math.sqrt(2.0 * math.pi))
    return normal_cdf + values * normal_pdf

def reference(tokens, targets, stem_half, conv_half, point_half, head_half):
    stem_full, conv_full, point_full, head_full = expand_weights(stem_half, conv_half, point_half, head_half)
    sequence_total, sequence_length, base_count = tokens.shape
    total_rows = sequence_total * sequence_length
    kernel_taps = conv_full.shape[0]
    channel_total = stem_full.shape[1]
    inner_features = conv_full.shape[2]
    receptive_bins = DILATION_STEP * (kernel_taps // 2)
    onehot = (tokens[..., None] == jnp.arange(4, dtype=jnp.int32)).astype(jnp.bfloat16).reshape(total_rows, 4 * base_count)
    embed = jnp.dot(onehot, stem_full, preferred_element_type=jnp.float32).astype(jnp.bfloat16)
    embed_wide = embed.astype(jnp.float32)
    inv_root = lax.rsqrt(lax.optimization_barrier(jnp.mean(embed_wide * embed_wide, axis=1, keepdims=True)) + 1e-05)
    normed_input = (embed_wide * inv_root).astype(jnp.bfloat16)
    padded_input = jnp.pad(normed_input.reshape(sequence_total, sequence_length, channel_total), ((0, 0), (receptive_bins, receptive_bins), (0, 0)))
    pre = jnp.zeros((total_rows, inner_features), jnp.float32)
    windows = []
    for kernel_tap_index in range(kernel_taps):
        sliding_window = padded_input[:, kernel_tap_index * DILATION_STEP:kernel_tap_index * DILATION_STEP + sequence_length].reshape(total_rows, channel_total)
        windows.append(sliding_window)
        pre = pre + jnp.dot(sliding_window, conv_full[kernel_tap_index], preferred_element_type=jnp.float32)
    activated = jax.nn.gelu(pre, approximate=False).astype(jnp.bfloat16)
    after = (embed_wide + jnp.dot(activated, point_full, preferred_element_type=jnp.float32)).astype(jnp.bfloat16)
    logits = jnp.dot(after, head_full, preferred_element_type=jnp.float32)
    scale = 1.0 / math.sqrt(total_rows)
    counts = targets.reshape(total_rows, -1).astype(jnp.float32)
    loss_grad = ((jnp.exp(logits) - counts) * scale).astype(jnp.bfloat16)
    half_c = channel_total // 2
    head_sum = jnp.dot(loss_grad.T, after, preferred_element_type=jnp.float32)
    grad_head = head_sum[:, :half_c] + head_sum[:, half_c:][:, ::-1]
    up_grad = jnp.dot(loss_grad, head_full.T, preferred_element_type=jnp.float32).astype(jnp.bfloat16)
    point_sum = jnp.dot(activated.T, up_grad, preferred_element_type=jnp.float32)
    grad_point = point_sum[:, :half_c] + point_sum[:, half_c:][::-1, ::-1]
    act_grad = jnp.dot(up_grad, point_full.T, preferred_element_type=jnp.float32)
    preactivation_gradient = (act_grad * gelu_slope(pre)).astype(jnp.bfloat16)
    conv_sum = jnp.stack([jnp.dot(windows[kernel_tap_index].T, preactivation_gradient, preferred_element_type=jnp.float32) for kernel_tap_index in range(kernel_taps)])
    half_h = inner_features // 2
    grad_conv = (conv_sum[..., :half_h] + conv_sum[..., half_h:][::-1, ::-1, ::-1]).reshape(kernel_taps * channel_total, half_h)
    padded_gradient = jnp.pad(preactivation_gradient.reshape(sequence_total, sequence_length, inner_features), ((0, 0), (receptive_bins, receptive_bins), (0, 0)))
    normed_grad = jnp.zeros((total_rows, channel_total), jnp.float32)
    for kernel_tap_index in range(kernel_taps):
        offset_begin = (kernel_taps - 1 - kernel_tap_index) * DILATION_STEP
        piece = padded_gradient[:, offset_begin:offset_begin + sequence_length].reshape(total_rows, inner_features)
        normed_grad = normed_grad + jnp.dot(piece, conv_full[kernel_tap_index].T, preferred_element_type=jnp.float32)
    inner_mean = lax.optimization_barrier(jnp.mean(normed_grad * embed_wide, axis=1, keepdims=True))
    embed_grad = (inv_root * normed_grad - embed_wide * inv_root * inv_root * inv_root * inner_mean + up_grad.astype(jnp.float32)).astype(jnp.bfloat16)
    stem_sum = jnp.dot(onehot.T, embed_grad, preferred_element_type=jnp.float32)
    grad_stem = stem_sum[:, :half_c] + stem_sum[:, half_c:][::-1, ::-1]
    return (grad_stem, grad_conv, grad_point, grad_head)
```

```python
import math

import jax
import jax.numpy as jnp
from jax import lax
from jax.sharding import PartitionSpec as P

DILATION_STEP = 128
BF = jnp.bfloat16
F32 = jnp.float32


def mm(a, b):
    return lax.dot_general(a, b, (((1,), (0,)), ((), ())), preferred_element_type=F32)


def mm_nt(a, b):
    return lax.dot_general(a, b, (((1,), (1,)), ((), ())), preferred_element_type=F32)


def mm_tn(a, b):
    return lax.dot_general(a, b, (((0,), (0,)), ((), ())), preferred_element_type=F32)


def exchange(size):
    row = lax.broadcasted_iota(jnp.int32, (size, size), 0)
    col = lax.broadcasted_iota(jnp.int32, (size, size), 1)
    return jnp.where(row + col == size - 1, 1.0, 0.0).astype(BF)


def onehots(marks):
    bases = marks.shape[1]
    row = lax.broadcasted_iota(jnp.int32, (bases, 4 * bases), 0)
    col = lax.broadcasted_iota(jnp.int32, (bases, 4 * bases), 1)
    spread = jnp.where(row == col // 4, 1.0, 0.0).astype(BF)
    spread_rev = jnp.where(bases - 1 - row == col // 4, 1.0, 0.0).astype(BF)
    base = (lax.broadcasted_iota(jnp.int32, (1, 4 * bases), 1) % 4).astype(F32)
    hot = jnp.where(mm(marks, spread) == base + 1.0, 1.0, 0.0).astype(BF)
    hot_rev = jnp.where(mm(marks, spread_rev) == 4.0 - base, 1.0, 0.0).astype(BF)
    return hot, hot_rev


def embed_rows(hot, hot_rev, stem_both, half_c):
    plain = mm(hot, stem_both).astype(BF)
    other = mm(hot_rev, stem_both).astype(BF)
    ordered = jnp.concatenate([plain[:, :half_c], other[:, half_c:]], axis=1)
    reverse = jnp.concatenate([other[:, :half_c], plain[:, half_c:]], axis=1)
    wide = ordered.astype(F32)
    inv_root = lax.rsqrt(jnp.mean(wide * wide, axis=1, keepdims=True) + 1e-05)
    normed = (wide * inv_root).astype(BF)
    normed_rev = (reverse.astype(F32) * inv_root).astype(BF)
    return ordered, reverse, inv_root, normed, normed_rev


def normal_cdf(values):
    return 0.5 * (1.0 + lax.erf(values * (1.0 / math.sqrt(2.0))))


def normal_pdf(values):
    return jnp.exp(-0.5 * values * values) * (1.0 / math.sqrt(2.0 * math.pi))


def halo(x, width):
    count = lax.axis_size("ctx")
    up = [(i, i + 1) for i in range(count - 1)]
    down = [(j, i) for i, j in up]
    before = lax.ppermute(x[x.shape[0] - width :], "ctx", up)
    after = lax.ppermute(x[:width], "ctx", down)
    return jnp.concatenate([before, x, after], axis=0)


def local(tokens, targets, stem, conv, point, head):
    ctx_count = lax.axis_size("ctx")
    dp_count = lax.axis_size("dp")
    rows = tokens.shape[1]
    taps = conv.shape[0]
    half_c, half_h = stem.shape[1], conv.shape[2]
    width = (taps // 2) * DILATION_STEP
    step = DILATION_STEP
    scale = 1.0 / math.sqrt(rows * ctx_count * dp_count)

    marks = halo((tokens[0] + 1).astype(BF), width)
    flip_c = exchange(half_c)
    flip_h = exchange(half_h)
    stem_both = jnp.concatenate([stem, mm(stem, flip_c).astype(BF)], axis=1)
    conv_low = [mm(flip_c, conv[k, half_c:]).astype(BF) for k in range(taps)]
    point_low = mm(flip_h, point[half_h:]).astype(BF)
    point_a = jnp.concatenate([point[:half_h], point_low], axis=1)
    point_b = jnp.concatenate([point_low, point[:half_h]], axis=1)
    head_both = jnp.concatenate([head, head], axis=0)

    hot, hot_rev = onehots(marks)
    ordered, reverse, inv_root, normed, normed_rev = embed_rows(hot, hot_rev, stem_both, half_c)
    mid = slice(width, width + rows)
    inv = inv_root[mid]
    embed = jnp.concatenate([ordered[mid, :half_c], reverse[mid, :half_c]], axis=1).astype(F32)

    def tap(x, k):
        return x[k * step : k * step + rows]

    pre_a = sum(mm(tap(normed, k), conv[k]) for k in range(taps))
    pre_b = sum(mm(tap(normed_rev, k), conv[taps - 1 - k]) for k in range(taps))
    pre = jnp.concatenate([pre_a, pre_b], axis=1)
    cdf = normal_cdf(pre)
    act = (pre * cdf).astype(BF)
    act_a, act_b = act[:, :half_h], act[:, half_h:]
    after = (embed + mm(act_a, point_a) + mm(act_b, point_b)).astype(BF)
    logits = mm(after, head_both)
    loss_grad = ((jnp.exp(logits) - targets[0].astype(F32)) * scale).astype(BF)
    up = mm_nt(loss_grad, head).astype(BF)
    up_both = jnp.concatenate([up, up], axis=1)
    act_grad = mm_nt(up_both, point_a)
    slope = cdf + pre * normal_pdf(pre)
    pre_grad = (jnp.concatenate([act_grad, act_grad], axis=1) * slope).astype(BF)
    pre_halo = halo(pre_grad, width)

    g_head = mm_tn(
        jnp.concatenate([loss_grad, loss_grad], axis=0),
        jnp.concatenate([after[:, :half_c], after[:, half_c:]], axis=0),
    )
    act_all = jnp.concatenate(
        [
            jnp.concatenate([act_a, mm(act_b, flip_h).astype(BF)], axis=1),
            jnp.concatenate([act_b, mm(act_a, flip_h).astype(BF)], axis=1),
        ],
        axis=0,
    )
    g_point = mm_tn(act_all, jnp.concatenate([up, up], axis=0))
    grads = jnp.concatenate([pre_grad[:, :half_h], pre_grad[:, half_h:]], axis=0)
    g_conv = jnp.concatenate(
        [
            mm_tn(jnp.concatenate([tap(normed, k), tap(normed_rev, taps - 1 - k)], axis=0), grads)
            for k in range(taps)
        ],
        axis=0,
    )
    normed_grad = jnp.zeros((rows, 2 * half_c), F32)
    for k in range(taps):
        piece = tap(pre_halo, taps - 1 - k)
        weight = jnp.concatenate(
            [
                jnp.concatenate([conv[k, :half_c], conv_low[taps - 1 - k]], axis=1),
                jnp.concatenate([conv_low[k], conv[taps - 1 - k, :half_c]], axis=1),
            ],
            axis=0,
        )
        normed_grad = normed_grad + mm_nt(piece, weight)
    inner = jnp.mean(normed_grad * embed, axis=1, keepdims=True)
    embed_grad = (
        inv * normed_grad - embed * inv * inv * inv * inner + up_both.astype(F32)
    ).astype(BF)
    g_stem = mm_tn(
        jnp.concatenate([hot[mid], hot_rev[mid]], axis=0),
        jnp.concatenate([embed_grad[:, :half_c], embed_grad[:, half_c:]], axis=0),
    )

    def reduce(term):
        blocks = term.reshape(ctx_count, dp_count, -1, term.shape[1])
        by_dp = lax.psum_scatter(jnp.swapaxes(blocks, 0, 1), "dp", scatter_dimension=0)
        return lax.psum_scatter(by_dp, "ctx", scatter_dimension=0)

    return reduce(g_stem), reduce(g_conv), reduce(g_point), reduce(g_head)


def solution(mesh):
    return jax.shard_map(
        local,
        mesh=mesh,
        in_specs=(
            P(("groups", "dp"), "ctx", None),
            P(("groups", "dp"), "ctx", None),
            P("groups", None),
            P("groups", None, None),
            P("groups", None),
            P("groups", None),
        ),
        out_specs=(P(("groups", "ctx", "dp"), None),) * 4,
        check_vma=False,
    )
```

```python
import functools
import math

import jax
import jax.numpy as jnp
from jax import lax
from jax.experimental import pallas as pl
from jax.experimental.pallas import tpu as pltpu
from jax.sharding import PartitionSpec as P

DILATION_STEP = 128
BF = jnp.bfloat16
F32 = jnp.float32


def mm(a, b):
    return lax.dot_general(a, b, (((1,), (0,)), ((), ())), preferred_element_type=F32)


def mm_nt(a, b):
    return lax.dot_general(a, b, (((1,), (1,)), ((), ())), preferred_element_type=F32)


def mm_tn(a, b):
    return lax.dot_general(a, b, (((0,), (0,)), ((), ())), preferred_element_type=F32)


def exchange(size):
    row = lax.broadcasted_iota(jnp.int32, (size, size), 0)
    col = lax.broadcasted_iota(jnp.int32, (size, size), 1)
    return jnp.where(row + col == size - 1, 1.0, 0.0).astype(BF)


def onehots(marks):
    bases = marks.shape[1]
    row = lax.broadcasted_iota(jnp.int32, (bases, 4 * bases), 0)
    col = lax.broadcasted_iota(jnp.int32, (bases, 4 * bases), 1)
    spread = jnp.where(row == lax.shift_right_logical(col, 2), 1.0, 0.0).astype(BF)
    spread_rev = jnp.where(bases - 1 - row == lax.shift_right_logical(col, 2), 1.0, 0.0).astype(BF)
    base = jnp.bitwise_and(lax.broadcasted_iota(jnp.int32, (1, 4 * bases), 1), 3).astype(F32)
    hot = jnp.where(mm(marks, spread) == base + 1.0, 1.0, 0.0).astype(BF)
    hot_rev = jnp.where(mm(marks, spread_rev) == 4.0 - base, 1.0, 0.0).astype(BF)
    return hot, hot_rev


def embed_rows(hot, hot_rev, stem_both, half_c):
    plain = mm(hot, stem_both).astype(BF)
    other = mm(hot_rev, stem_both).astype(BF)
    ordered = jnp.concatenate([plain[:, :half_c], other[:, half_c:]], axis=1)
    reverse = jnp.concatenate([other[:, :half_c], plain[:, half_c:]], axis=1)
    wide = ordered.astype(F32)
    inv_root = lax.rsqrt(jnp.mean(wide * wide, axis=1, keepdims=True) + 1e-05)
    normed = (wide * inv_root).astype(BF)
    normed_rev = (reverse.astype(F32) * inv_root).astype(BF)
    return ordered, reverse, inv_root, normed, normed_rev


def normal_cdf(values):
    return 0.5 * (1.0 + lax.erf(values * (1.0 / math.sqrt(2.0))))


def normal_pdf(values):
    return jnp.exp(-0.5 * values * values) * (1.0 / math.sqrt(2.0 * math.pi))


def halo(x, width):
    count = lax.axis_size("ctx")
    up = [(i, i + 1) for i in range(count - 1)]
    down = [(j, i) for i, j in up]
    before = lax.ppermute(x[x.shape[0] - width :], "ctx", up)
    after = lax.ppermute(x[:width], "ctx", down)
    return jnp.concatenate([before, x, after], axis=0)


def plain(tokens, targets, stem, conv, point, head):
    ctx_count = lax.axis_size("ctx")
    dp_count = lax.axis_size("dp")
    rows = tokens.shape[1]
    taps = conv.shape[0]
    half_c, half_h = stem.shape[1], conv.shape[2]
    width = (taps // 2) * DILATION_STEP
    step = DILATION_STEP
    scale = 1.0 / math.sqrt(rows * ctx_count * dp_count)

    marks = halo((tokens[0] + 1).astype(BF), width)
    flip_c = exchange(half_c)
    flip_h = exchange(half_h)
    stem_both = jnp.concatenate([stem, mm(stem, flip_c).astype(BF)], axis=1)
    conv_low = [mm(flip_c, conv[k, half_c:]).astype(BF) for k in range(taps)]
    point_low = mm(flip_h, point[half_h:]).astype(BF)
    point_a = jnp.concatenate([point[:half_h], point_low], axis=1)
    point_b = jnp.concatenate([point_low, point[:half_h]], axis=1)
    head_both = jnp.concatenate([head, head], axis=0)

    hot, hot_rev = onehots(marks)
    ordered, reverse, inv_root, normed, normed_rev = embed_rows(hot, hot_rev, stem_both, half_c)
    mid = slice(width, width + rows)
    inv = inv_root[mid]
    embed = jnp.concatenate([ordered[mid, :half_c], reverse[mid, :half_c]], axis=1).astype(F32)

    def tap(x, k):
        return x[k * step : k * step + rows]

    pre_a = sum(mm(tap(normed, k), conv[k]) for k in range(taps))
    pre_b = sum(mm(tap(normed_rev, k), conv[taps - 1 - k]) for k in range(taps))
    pre = jnp.concatenate([pre_a, pre_b], axis=1)
    cdf = normal_cdf(pre)
    act = (pre * cdf).astype(BF)
    act_a, act_b = act[:, :half_h], act[:, half_h:]
    after = (embed + mm(act_a, point_a) + mm(act_b, point_b)).astype(BF)
    logits = mm(after, head_both)
    loss_grad = ((jnp.exp(logits) - targets[0].astype(F32)) * scale).astype(BF)
    up = mm_nt(loss_grad, head).astype(BF)
    up_both = jnp.concatenate([up, up], axis=1)
    act_grad = mm_nt(up_both, point_a)
    slope = cdf + pre * normal_pdf(pre)
    pre_grad = (jnp.concatenate([act_grad, act_grad], axis=1) * slope).astype(BF)
    pre_halo = halo(pre_grad, width)

    g_head = mm_tn(
        jnp.concatenate([loss_grad, loss_grad], axis=0),
        jnp.concatenate([after[:, :half_c], after[:, half_c:]], axis=0),
    )
    act_all = jnp.concatenate(
        [
            jnp.concatenate([act_a, mm(act_b, flip_h).astype(BF)], axis=1),
            jnp.concatenate([act_b, mm(act_a, flip_h).astype(BF)], axis=1),
        ],
        axis=0,
    )
    g_point = mm_tn(act_all, jnp.concatenate([up, up], axis=0))
    grads = jnp.concatenate([pre_grad[:, :half_h], pre_grad[:, half_h:]], axis=0)
    g_conv = jnp.concatenate(
        [
            mm_tn(jnp.concatenate([tap(normed, k), tap(normed_rev, taps - 1 - k)], axis=0), grads)
            for k in range(taps)
        ],
        axis=0,
    )
    normed_grad = jnp.zeros((rows, 2 * half_c), F32)
    for k in range(taps):
        piece = tap(pre_halo, taps - 1 - k)
        weight = jnp.concatenate(
            [
                jnp.concatenate([conv[k, :half_c], conv_low[taps - 1 - k]], axis=1),
                jnp.concatenate([conv_low[k], conv[taps - 1 - k, :half_c]], axis=1),
            ],
            axis=0,
        )
        normed_grad = normed_grad + mm_nt(piece, weight)
    inner = jnp.mean(normed_grad * embed, axis=1, keepdims=True)
    embed_grad = (
        inv * normed_grad - embed * inv * inv * inv * inner + up_both.astype(F32)
    ).astype(BF)
    g_stem = mm_tn(
        jnp.concatenate([hot[mid], hot_rev[mid]], axis=0),
        jnp.concatenate([embed_grad[:, :half_c], embed_grad[:, half_c:]], axis=0),
    )

    def reduce(term):
        blocks = term.reshape(ctx_count, dp_count, -1, term.shape[1])
        by_dp = lax.psum_scatter(jnp.swapaxes(blocks, 0, 1), "dp", scatter_dimension=0)
        return lax.psum_scatter(by_dp, "ctx", scatter_dimension=0)

    return reduce(g_stem), reduce(g_conv), reduce(g_point), reduce(g_head)

MESH = pl.DeviceIdType.MESH


def up16(rows):
    return -(-rows // 16) * 16


def encode(values, out, slot):
    rows, cols = values.shape
    largest = jnp.maximum(jnp.max(jnp.abs(values), axis=0, keepdims=True), 1e-30)
    power = jnp.ceil(jnp.log2(largest))
    scaled = jnp.clip(jnp.round(values * jnp.exp2(15.0 - power)), -32767.0, 32767.0)
    out[slot, 0:rows] = scaled.astype(jnp.int32).astype(jnp.int16)
    tail = jnp.broadcast_to(power, (16, cols)).astype(jnp.int32).astype(jnp.int16)
    out[slot, up16(rows) : up16(rows) + 16] = tail


def decode(ref, slot, rows):
    values = ref[slot, 0:rows].astype(jnp.int32).astype(F32)
    power = ref[slot, up16(rows) : up16(rows) + 16].astype(jnp.int32).astype(F32)[0:1]
    return values * jnp.exp2(power - 15.0)


def kernel(ctx_count, dp_count, chunks, *refs):
    tokens, targets, stem, conv, point, head = refs[:6]
    o_stem, o_conv, o_point, o_head = refs[6:10]
    marks, pre_grads, normed, normed_rev, conv_low = refs[10:15]
    count = len(chunks)
    grad = refs[15 : 15 + count]
    from_core = refs[15 + count : 15 + 2 * count]
    to_x = refs[15 + 2 * count : 15 + 3 * count]
    from_x = refs[15 + 3 * count : 15 + 4 * count]
    to_z = refs[15 + 4 * count : 15 + 5 * count]
    from_z = refs[15 + 5 * count : 15 + 6 * count]
    (halo_send, halo_recv, core_send, core_recv, x_send, x_recv, z_send, z_recv) = refs[15 + 6 * count :]

    group = lax.axis_index("groups")
    ctx = lax.axis_index("ctx")
    dp = lax.axis_index("dp")
    core = lax.rem(dp, 2)
    side = dp // 2
    sibling = (group, ctx, dp + 1 - 2 * core)
    across = (group, ctx, lax.rem(dp + 2, dp_count))

    def along(distance):
        return (group, lax.rem(ctx + distance, ctx_count), dp)

    rows = tokens.shape[1]
    taps = conv.shape[0]
    half_c, half_h = stem.shape[1], conv.shape[2]
    width = (taps // 2) * DILATION_STEP
    step = DILATION_STEP
    mid = slice(width, width + rows)
    scale = 1.0 / math.sqrt(rows * ctx_count * dp_count)

    def zero_ends(buffer):
        zeros = jnp.zeros((width, buffer.shape[1]), buffer.dtype)

        @pl.when(ctx == 0)
        def _():
            buffer[0:width] = zeros

        @pl.when(ctx == ctx_count - 1)
        def _():
            buffer[width + rows : 2 * width + rows] = zeros

    def halo_copies(buffer, kind):
        upward = pltpu.make_async_remote_copy(
            src_ref=buffer.at[rows : rows + width],
            dst_ref=buffer.at[0:width],
            send_sem=halo_send.at[2 * kind],
            recv_sem=halo_recv.at[2 * kind],
            device_id=along(1),
            device_id_type=MESH,
        )
        downward = pltpu.make_async_remote_copy(
            src_ref=buffer.at[width : 2 * width],
            dst_ref=buffer.at[width + rows : 2 * width + rows],
            send_sem=halo_send.at[2 * kind + 1],
            recv_sem=halo_recv.at[2 * kind + 1],
            device_id=along(ctx_count - 1),
            device_id_type=MESH,
        )
        return upward, downward

    def halo_start(buffer, kind):
        upward, downward = halo_copies(buffer, kind)
        pl.when(ctx < ctx_count - 1)(upward.start)
        pl.when(ctx > 0)(downward.start)

    def halo_wait(buffer, kind):
        upward, downward = halo_copies(buffer, kind)
        pl.when(ctx > 0)(upward.wait_recv)
        pl.when(ctx < ctx_count - 1)(downward.wait_recv)

    def halo_sent(buffer, kind):
        upward, downward = halo_copies(buffer, kind)
        pl.when(ctx < ctx_count - 1)(upward.wait_send)
        pl.when(ctx > 0)(downward.wait_send)

    def core_copy(c):
        return pltpu.make_async_remote_copy(
            src_ref=grad[c].at[:, 1 - core],
            dst_ref=from_core[c],
            send_sem=core_send.at[c],
            recv_sem=core_recv.at[c],
            device_id=sibling,
            device_id_type=MESH,
        )

    def x_copy(c):
        return pltpu.make_async_remote_copy(
            src_ref=to_x[c],
            dst_ref=from_x[c],
            send_sem=x_send.at[c],
            recv_sem=x_recv.at[c],
            device_id=across,
            device_id_type=MESH,
        )

    def z_copy(c, distance):
        return pltpu.make_async_remote_copy(
            src_ref=to_z[c].at[distance - 1],
            dst_ref=from_z[c].at[distance - 1],
            send_sem=z_send.at[c * (ctx_count - 1) + distance - 1],
            recv_sem=z_recv.at[c * (ctx_count - 1) + distance - 1],
            device_id=along(distance),
            device_id_type=MESH,
        )

    def x_stage(c):
        core_copy(c).wait_recv()

        @pl.loop(0, ctx_count)
        def _(i):
            n = 2 * i + 1 - side
            encode(grad[c][n, core] + from_core[c][n], to_x[c], i)

        x_copy(c).start()

    def chip_sum(c, i):
        n = 2 * i + side
        return grad[c][n, core] + from_core[c][n] + decode(from_x[c], i, chunks[c][0])

    def z_stage(c):
        x_copy(c).wait_recv()
        for distance in range(1, ctx_count):
            encode(chip_sum(c, lax.rem(ctx + distance, ctx_count)), to_z[c], distance - 1)
            z_copy(c, distance).start()

    def last_stage(c):
        total = chip_sum(c, ctx)
        for distance in range(1, ctx_count):
            z_copy(c, distance).wait_recv()
            total = total + decode(from_z[c], distance - 1, chunks[c][0])
        return total

    marks[mid] = (tokens[0] + 1).astype(F32).astype(BF)
    zero_ends(marks)
    zero_ends(pre_grads)
    barrier = pltpu.get_barrier_semaphore()
    partners = [sibling, across] + [along(d) for d in range(1, ctx_count)]
    for partner in partners:
        pl.semaphore_signal(barrier, inc=1, device_id=partner, device_id_type=MESH)
    pl.semaphore_wait(barrier, len(partners))
    halo_start(marks, 0)

    flip_c = exchange(half_c)
    flip_h = exchange(half_h)
    stem_both = jnp.concatenate([stem[...], mm(stem[...], flip_c).astype(BF)], axis=1)
    for k in range(taps):
        conv_low[k] = mm(flip_c, conv[k, half_c:]).astype(BF)
    point_high = point[0:half_h]
    point_low = mm(flip_h, point[half_h:]).astype(BF)
    point_a = jnp.concatenate([point_high, point_low], axis=1)
    point_b = jnp.concatenate([point_low, point_high], axis=1)

    def embed_part(start, size):
        part = slice(start, start + size)
        hot, hot_rev = onehots(marks[part])
        ordered, reverse, inv, one, other = embed_rows(hot, hot_rev, stem_both, half_c)
        normed[part] = one
        normed_rev[part] = other
        return hot, hot_rev, ordered, reverse, inv

    hot, hot_rev, ordered, reverse, inv = embed_part(width, rows)
    embed = jnp.concatenate([ordered[:, :half_c], reverse[:, :half_c]], axis=1).astype(F32)
    halo_wait(marks, 0)
    embed_part(0, width)
    embed_part(width + rows, width)

    def tap(ref, k):
        return ref[k * step : k * step + rows]

    pre_a = sum(mm(tap(normed, k), conv[k]) for k in range(taps))
    pre_b = sum(mm(tap(normed_rev, k), conv[taps - 1 - k]) for k in range(taps))
    pre = jnp.concatenate([pre_a, pre_b], axis=1)
    cdf = normal_cdf(pre)
    act = (pre * cdf).astype(BF)
    slope = cdf + pre * normal_pdf(pre)
    act_a, act_b = act[:, :half_h], act[:, half_h:]
    after = (embed + mm(act_a, point_a) + mm(act_b, point_b)).astype(BF)
    head_both = jnp.concatenate([head[...], head[...]], axis=0)
    logits = mm(after, head_both)
    loss_grad = ((jnp.exp(logits) - targets[0].astype(F32)) * scale).astype(BF)
    up = mm_nt(loss_grad, head[...]).astype(BF)
    up_both = jnp.concatenate([up, up], axis=1)
    act_grad = mm_nt(up_both, point_a)
    pre_grad = (jnp.concatenate([act_grad, act_grad], axis=1) * slope).astype(BF)
    pre_grads[mid] = pre_grad
    halo_start(pre_grads, 1)

    blocks = ctx_count * dp_count
    head_rows, point_rows = o_head.shape[0], o_point.shape[0]
    g_head = mm_tn(
        jnp.concatenate([loss_grad, loss_grad], axis=0),
        jnp.concatenate([after[:, :half_c], after[:, half_c:]], axis=0),
    )
    for n in range(blocks):
        grad[0][n // 2, n % 2, 0:head_rows] = g_head[n * head_rows : (n + 1) * head_rows]
    act_all = jnp.concatenate(
        [
            jnp.concatenate([act_a, mm(act_b, flip_h).astype(BF)], axis=1),
            jnp.concatenate([act_b, mm(act_a, flip_h).astype(BF)], axis=1),
        ],
        axis=0,
    )
    g_point = mm_tn(act_all, jnp.concatenate([up, up], axis=0))
    for n in range(blocks):
        grad[0][n // 2, n % 2, head_rows : head_rows + point_rows] = g_point[
            n * point_rows : (n + 1) * point_rows
        ]
    core_copy(0).start()

    conv_rows = o_conv.shape[0]
    conv_cols = chunks[1][1]
    grads = jnp.concatenate([pre_grad[:, :half_h], pre_grad[:, half_h:]], axis=0)
    for k in range(taps):
        both = jnp.concatenate([tap(normed, k), tap(normed_rev, taps - 1 - k)], axis=0)
        term = mm_tn(both, grads)
        first, end = k * 2 * half_c, (k + 1) * 2 * half_c
        at = first
        while at < end:
            n = at // conv_rows
            stop = min(end, (n + 1) * conv_rows)
            for c in range(half_h // conv_cols):
                grad[1 + c][n // 2, n % 2, at - n * conv_rows : stop - n * conv_rows] = term[
                    at - first : stop - first, c * conv_cols : (c + 1) * conv_cols
                ]
            at = stop
    core_copy(1).start()
    core_copy(2).start()
    x_stage(0)
    x_stage(1)
    x_stage(2)

    halo_wait(pre_grads, 1)
    normed_grad = jnp.zeros((rows, 2 * half_c), F32)
    for k in range(taps):
        weight = jnp.concatenate(
            [
                jnp.concatenate([conv[k, 0:half_c], conv_low[taps - 1 - k]], axis=1),
                jnp.concatenate([conv_low[k], conv[taps - 1 - k, 0:half_c]], axis=1),
            ],
            axis=0,
        )
        normed_grad = normed_grad + mm_nt(tap(pre_grads, taps - 1 - k), weight)
    inner = jnp.mean(normed_grad * embed, axis=1, keepdims=True)
    embed_grad = (
        inv * normed_grad - embed * inv * inv * inv * inner + up_both.astype(F32)
    ).astype(BF)
    g_stem = mm_tn(
        jnp.concatenate([hot, hot_rev], axis=0),
        jnp.concatenate([embed_grad[:, :half_c], embed_grad[:, half_c:]], axis=0),
    )
    stem_rows = o_stem.shape[0]
    for n in range(blocks):
        grad[3][n // 2, n % 2] = g_stem[n * stem_rows : (n + 1) * stem_rows]
    core_copy(3).start()

    z_stage(0)
    x_stage(3)
    z_stage(1)
    z_stage(2)
    z_stage(3)
    total = last_stage(0)
    o_head[...] = total[0:head_rows]
    o_point[...] = total[head_rows : head_rows + point_rows]
    o_conv[:, 0:conv_cols] = last_stage(1)
    o_conv[:, conv_cols : 2 * conv_cols] = last_stage(2)
    o_stem[...] = last_stage(3)

    halo_sent(marks, 0)
    halo_sent(pre_grads, 1)
    for c in range(count):
        core_copy(c).wait_send()
        x_copy(c).wait_send()
        for distance in range(1, ctx_count):
            z_copy(c, distance).wait_send()


def local(tokens, targets, stem, conv, point, head):
    ctx_count = lax.axis_size("ctx")
    dp_count = lax.axis_size("dp")
    rows = tokens.shape[1]
    taps = conv.shape[0]
    half_c, half_h = stem.shape[1], conv.shape[2]
    width = (taps // 2) * DILATION_STEP
    blocks = ctx_count * dp_count
    totals = (stem.shape[0], taps * 2 * half_c, point.shape[0], head.shape[1])
    fits = all(total % (8 * blocks) == 0 for total in totals)
    if not (fits and dp_count == 4 and 2 <= ctx_count <= 4 and rows >= width and tokens.shape[0] == 1):
        return plain(tokens, targets, stem, conv, point, head)
    out_rows = [total // blocks for total in totals]
    chunks = (
        (out_rows[3] + out_rows[2], half_c),
        (out_rows[1], half_h // 2),
        (out_rows[1], half_h // 2),
        (out_rows[0], half_c),
    )
    vmem = pl.BlockSpec(memory_space=pltpu.VMEM)
    scratch = [
        pltpu.VMEM((rows + 2 * width, tokens.shape[2]), BF),
        pltpu.VMEM((rows + 2 * width, 2 * half_h), BF),
        pltpu.VMEM((rows + 2 * width, 2 * half_c), BF),
        pltpu.VMEM((rows + 2 * width, 2 * half_c), BF),
        pltpu.VMEM((taps, half_c, half_h), BF),
    ]
    scratch += [pltpu.VMEM((blocks // 2, 2, r, c), F32) for r, c in chunks]
    scratch += [pltpu.VMEM((blocks // 2, r, c), F32) for r, c in chunks]
    for slots in (ctx_count, ctx_count, ctx_count - 1, ctx_count - 1):
        scratch += [pltpu.VMEM((slots, up16(r) + 16, c), jnp.int16) for r, c in chunks]
    dma = pltpu.SemaphoreType.DMA
    count = len(chunks)
    scratch += [dma((4,)), dma((4,))]
    scratch += [dma((count,)) for _ in range(4)]
    scratch += [dma((count * (ctx_count - 1),)) for _ in range(2)]
    return pl.pallas_call(
        functools.partial(kernel, ctx_count, dp_count, chunks),
        out_shape=(
            jax.ShapeDtypeStruct((out_rows[0], half_c), F32),
            jax.ShapeDtypeStruct((out_rows[1], half_h), F32),
            jax.ShapeDtypeStruct((out_rows[2], half_c), F32),
            jax.ShapeDtypeStruct((out_rows[3], half_c), F32),
        ),
        in_specs=[vmem] * 6,
        out_specs=(vmem,) * 4,
        scratch_shapes=scratch,
        compiler_params=pltpu.CompilerParams(
            collective_id=0, has_side_effects=True, vmem_limit_bytes=56 * 1024 * 1024
        ),
        name="step",
    )(tokens, targets, stem, conv, point, head)


def solution(mesh):
    return jax.shard_map(
        local,
        mesh=mesh,
        in_specs=(
            P(("groups", "dp"), "ctx", None),
            P(("groups", "dp"), "ctx", None),
            P("groups", None),
            P("groups", None, None),
            P("groups", None),
            P("groups", None),
        ),
        out_specs=(P(("groups", "ctx", "dp"), None),) * 4,
        check_vma=False,
    )
```

```python
import functools
import math

import jax
import jax.numpy as jnp
from jax import lax
from jax.experimental import pallas as pl
from jax.experimental.pallas import tpu as pltpu
from jax.sharding import PartitionSpec as P

DILATION_STEP = 128
BF = jnp.bfloat16
F32 = jnp.float32


def mm(a, b):
    return lax.dot_general(a, b, (((1,), (0,)), ((), ())), preferred_element_type=F32)


def mm_nt(a, b):
    return lax.dot_general(a, b, (((1,), (1,)), ((), ())), preferred_element_type=F32)


def mm_tn(a, b):
    return lax.dot_general(a, b, (((0,), (0,)), ((), ())), preferred_element_type=F32)


def exchange(size):
    row = lax.broadcasted_iota(jnp.int32, (size, size), 0)
    col = lax.broadcasted_iota(jnp.int32, (size, size), 1)
    return jnp.where(row + col == size - 1, 1.0, 0.0).astype(BF)


def onehots(marks):
    bases = marks.shape[1]
    row = lax.broadcasted_iota(jnp.int32, (bases, 4 * bases), 0)
    col = lax.broadcasted_iota(jnp.int32, (bases, 4 * bases), 1)
    spread = jnp.where(row == lax.shift_right_logical(col, 2), 1.0, 0.0).astype(BF)
    spread_rev = jnp.where(bases - 1 - row == lax.shift_right_logical(col, 2), 1.0, 0.0).astype(BF)
    base = jnp.bitwise_and(lax.broadcasted_iota(jnp.int32, (1, 4 * bases), 1), 3).astype(F32)
    hot = jnp.where(mm(marks, spread) == base + 1.0, 1.0, 0.0).astype(BF)
    hot_rev = jnp.where(mm(marks, spread_rev) == 4.0 - base, 1.0, 0.0).astype(BF)
    return hot, hot_rev


def embed_rows(hot, hot_rev, stem_both, half_c):
    plain = mm(hot, stem_both).astype(BF)
    other = mm(hot_rev, stem_both).astype(BF)
    ordered = jnp.concatenate([plain[:, :half_c], other[:, half_c:]], axis=1)
    reverse = jnp.concatenate([other[:, :half_c], plain[:, half_c:]], axis=1)
    wide = ordered.astype(F32)
    inv_root = lax.rsqrt(jnp.mean(wide * wide, axis=1, keepdims=True) + 1e-05)
    normed = (wide * inv_root).astype(BF)
    normed_rev = (reverse.astype(F32) * inv_root).astype(BF)
    return ordered, reverse, inv_root, normed, normed_rev


def normal_cdf(values):
    return 0.5 * (1.0 + lax.erf(values * (1.0 / math.sqrt(2.0))))


def normal_pdf(values):
    return jnp.exp(-0.5 * values * values) * (1.0 / math.sqrt(2.0 * math.pi))


def halo(x, width):
    count = lax.axis_size("ctx")
    up = [(i, i + 1) for i in range(count - 1)]
    down = [(j, i) for i, j in up]
    before = lax.ppermute(x[x.shape[0] - width :], "ctx", up)
    after = lax.ppermute(x[:width], "ctx", down)
    return jnp.concatenate([before, x, after], axis=0)


def plain(tokens, targets, stem, conv, point, head):
    ctx_count = lax.axis_size("ctx")
    dp_count = lax.axis_size("dp")
    rows = tokens.shape[1]
    taps = conv.shape[0]
    half_c, half_h = stem.shape[1], conv.shape[2]
    width = (taps // 2) * DILATION_STEP
    step = DILATION_STEP
    scale = 1.0 / math.sqrt(rows * ctx_count * dp_count)

    marks = halo((tokens[0] + 1).astype(BF), width)
    flip_c = exchange(half_c)
    flip_h = exchange(half_h)
    stem_both = jnp.concatenate([stem, mm(stem, flip_c).astype(BF)], axis=1)
    conv_low = [mm(flip_c, conv[k, half_c:]).astype(BF) for k in range(taps)]
    point_low = mm(flip_h, point[half_h:]).astype(BF)
    point_a = jnp.concatenate([point[:half_h], point_low], axis=1)
    point_b = jnp.concatenate([point_low, point[:half_h]], axis=1)
    head_both = jnp.concatenate([head, head], axis=0)

    hot, hot_rev = onehots(marks)
    ordered, reverse, inv_root, normed, normed_rev = embed_rows(hot, hot_rev, stem_both, half_c)
    mid = slice(width, width + rows)
    inv = inv_root[mid]
    embed = jnp.concatenate([ordered[mid, :half_c], reverse[mid, :half_c]], axis=1).astype(F32)

    def tap(x, k):
        return x[k * step : k * step + rows]

    pre_a = sum(mm(tap(normed, k), conv[k]) for k in range(taps))
    pre_b = sum(mm(tap(normed_rev, k), conv[taps - 1 - k]) for k in range(taps))
    pre = jnp.concatenate([pre_a, pre_b], axis=1)
    cdf = normal_cdf(pre)
    act = (pre * cdf).astype(BF)
    act_a, act_b = act[:, :half_h], act[:, half_h:]
    after = (embed + mm(act_a, point_a) + mm(act_b, point_b)).astype(BF)
    logits = mm(after, head_both)
    loss_grad = ((jnp.exp(logits) - targets[0].astype(F32)) * scale).astype(BF)
    up = mm_nt(loss_grad, head).astype(BF)
    up_both = jnp.concatenate([up, up], axis=1)
    act_grad = mm_nt(up_both, point_a)
    slope = cdf + pre * normal_pdf(pre)
    pre_grad = (jnp.concatenate([act_grad, act_grad], axis=1) * slope).astype(BF)
    pre_halo = halo(pre_grad, width)

    g_head = mm_tn(
        jnp.concatenate([loss_grad, loss_grad], axis=0),
        jnp.concatenate([after[:, :half_c], after[:, half_c:]], axis=0),
    )
    act_all = jnp.concatenate(
        [
            jnp.concatenate([act_a, mm(act_b, flip_h).astype(BF)], axis=1),
            jnp.concatenate([act_b, mm(act_a, flip_h).astype(BF)], axis=1),
        ],
        axis=0,
    )
    g_point = mm_tn(act_all, jnp.concatenate([up, up], axis=0))
    grads = jnp.concatenate([pre_grad[:, :half_h], pre_grad[:, half_h:]], axis=0)
    g_conv = jnp.concatenate(
        [
            mm_tn(jnp.concatenate([tap(normed, k), tap(normed_rev, taps - 1 - k)], axis=0), grads)
            for k in range(taps)
        ],
        axis=0,
    )
    normed_grad = jnp.zeros((rows, 2 * half_c), F32)
    for k in range(taps):
        piece = tap(pre_halo, taps - 1 - k)
        weight = jnp.concatenate(
            [
                jnp.concatenate([conv[k, :half_c], conv_low[taps - 1 - k]], axis=1),
                jnp.concatenate([conv_low[k], conv[taps - 1 - k, :half_c]], axis=1),
            ],
            axis=0,
        )
        normed_grad = normed_grad + mm_nt(piece, weight)
    inner = jnp.mean(normed_grad * embed, axis=1, keepdims=True)
    embed_grad = (
        inv * normed_grad - embed * inv * inv * inv * inner + up_both.astype(F32)
    ).astype(BF)
    g_stem = mm_tn(
        jnp.concatenate([hot[mid], hot_rev[mid]], axis=0),
        jnp.concatenate([embed_grad[:, :half_c], embed_grad[:, half_c:]], axis=0),
    )

    def reduce(term):
        blocks = term.reshape(ctx_count, dp_count, -1, term.shape[1])
        by_dp = lax.psum_scatter(jnp.swapaxes(blocks, 0, 1), "dp", scatter_dimension=0)
        return lax.psum_scatter(by_dp, "ctx", scatter_dimension=0)

    return reduce(g_stem), reduce(g_conv), reduce(g_point), reduce(g_head)

MESH = pl.DeviceIdType.MESH


def packed_rows(rows, cols):
    return -(-(cols // 128 * rows + 8) // 16) * 16


def encode(values, out, slot):
    rows, cols = values.shape
    groups = cols // 128
    tail = packed_rows(rows, cols) - groups * rows
    largest = jnp.maximum(jnp.max(jnp.abs(values), axis=0, keepdims=True), 1e-30)
    power = jnp.ceil(jnp.log2(largest))
    scaled = jnp.clip(jnp.round(values * jnp.exp2(15.0 - power)), -32767.0, 32767.0)
    line = lax.broadcasted_iota(jnp.int32, (tail, 128), 0)
    last = jnp.zeros((tail, 128), F32)
    pieces = []
    for g in range(groups):
        lanes = slice(g * 128, (g + 1) * 128)
        pieces.append(scaled[:, lanes])
        last = jnp.where(line == g, power[:, lanes], last)
    out[slot] = jnp.concatenate(pieces + [last], axis=0).astype(jnp.int32).astype(jnp.int16)


def decode(ref, slot, rows, cols):
    values = ref[slot].astype(jnp.int32).astype(F32)
    groups = cols // 128
    last = groups * rows
    pieces = []
    for g in range(groups):
        power = values[last + g : last + g + 1]
        pieces.append(values[g * rows : (g + 1) * rows] * jnp.exp2(power - 15.0))
    return pieces[0] if groups == 1 else jnp.concatenate(pieces, axis=1)


def kernel(ctx_count, dp_count, chunks, *refs):
    tokens, targets, stem, conv, point, head = refs[:6]
    o_stem, o_conv, o_point, o_head = refs[6:10]
    marks, pre_grads, normed, normed_rev, conv_low = refs[10:15]
    count = len(chunks)
    grad = refs[15 : 15 + count]
    from_core = refs[15 + count : 15 + 2 * count]
    to_x = refs[15 + 2 * count : 15 + 3 * count]
    from_x = refs[15 + 3 * count : 15 + 4 * count]
    to_z = refs[15 + 4 * count : 15 + 5 * count]
    from_z = refs[15 + 5 * count : 15 + 6 * count]
    (halo_send, halo_recv, core_send, core_recv, x_send, x_recv, z_send, z_recv) = refs[15 + 6 * count :]

    group = lax.axis_index("groups")
    ctx = lax.axis_index("ctx")
    dp = lax.axis_index("dp")
    core = lax.rem(dp, 2)
    side = dp // 2
    sibling = (group, ctx, dp + 1 - 2 * core)
    across = (group, ctx, lax.rem(dp + 2, dp_count))

    def along(distance):
        return (group, lax.rem(ctx + distance, ctx_count), dp)

    rows = tokens.shape[1]
    taps = conv.shape[0]
    half_c, half_h = stem.shape[1], conv.shape[2]
    width = (taps // 2) * DILATION_STEP
    step = DILATION_STEP
    mid = slice(width, width + rows)
    scale = 1.0 / math.sqrt(rows * ctx_count * dp_count)

    def zero_ends(buffer):
        zeros = jnp.zeros((width, buffer.shape[1]), buffer.dtype)

        @pl.when(ctx == 0)
        def _():
            buffer[0:width] = zeros

        @pl.when(ctx == ctx_count - 1)
        def _():
            buffer[width + rows : 2 * width + rows] = zeros

    def halo_copies(buffer, kind):
        upward = pltpu.make_async_remote_copy(
            src_ref=buffer.at[rows : rows + width],
            dst_ref=buffer.at[0:width],
            send_sem=halo_send.at[2 * kind],
            recv_sem=halo_recv.at[2 * kind],
            device_id=along(1),
            device_id_type=MESH,
        )
        downward = pltpu.make_async_remote_copy(
            src_ref=buffer.at[width : 2 * width],
            dst_ref=buffer.at[width + rows : 2 * width + rows],
            send_sem=halo_send.at[2 * kind + 1],
            recv_sem=halo_recv.at[2 * kind + 1],
            device_id=along(ctx_count - 1),
            device_id_type=MESH,
        )
        return upward, downward

    def halo_start(buffer, kind):
        upward, downward = halo_copies(buffer, kind)
        pl.when(ctx < ctx_count - 1)(upward.start)
        pl.when(ctx > 0)(downward.start)

    def halo_wait(buffer, kind):
        upward, downward = halo_copies(buffer, kind)
        pl.when(ctx > 0)(upward.wait_recv)
        pl.when(ctx < ctx_count - 1)(downward.wait_recv)

    def halo_sent(buffer, kind):
        upward, downward = halo_copies(buffer, kind)
        pl.when(ctx < ctx_count - 1)(upward.wait_send)
        pl.when(ctx > 0)(downward.wait_send)

    def core_copy(c):
        return pltpu.make_async_remote_copy(
            src_ref=grad[c].at[:, 1 - core],
            dst_ref=from_core[c],
            send_sem=core_send.at[c],
            recv_sem=core_recv.at[c],
            device_id=sibling,
            device_id_type=MESH,
        )

    def x_copy(c, slot):
        return pltpu.make_async_remote_copy(
            src_ref=to_x[c].at[slot],
            dst_ref=from_x[c].at[slot],
            send_sem=x_send.at[c * ctx_count + slot],
            recv_sem=x_recv.at[c * ctx_count + slot],
            device_id=across,
            device_id_type=MESH,
        )

    def z_copy(c, distance):
        return pltpu.make_async_remote_copy(
            src_ref=to_z[c].at[distance - 1],
            dst_ref=from_z[c].at[distance - 1],
            send_sem=z_send.at[c * (ctx_count - 1) + distance - 1],
            recv_sem=z_recv.at[c * (ctx_count - 1) + distance - 1],
            device_id=along(distance),
            device_id_type=MESH,
        )

    def x_stage(c):
        core_copy(c).wait_recv()
        for slot in range(ctx_count):
            n = 2 * lax.rem(ctx + 1 + slot, ctx_count) + 1 - side
            encode(grad[c][n, core] + from_core[c][n], to_x[c], slot)
            x_copy(c, slot).start()

    def chip_sum(c, slot):
        x_copy(c, slot).wait_recv()
        n = 2 * lax.rem(ctx + 1 + slot, ctx_count) + side
        return grad[c][n, core] + from_core[c][n] + decode(from_x[c], slot, *chunks[c])

    def z_part(c, distance):
        encode(chip_sum(c, distance - 1), to_z[c], distance - 1)
        z_copy(c, distance).start()

    def z_stage(c):
        for distance in range(1, ctx_count):
            z_part(c, distance)

    def last_stage(c):
        total = chip_sum(c, ctx_count - 1)
        for distance in range(1, ctx_count):
            z_copy(c, distance).wait_recv()
            total = total + decode(from_z[c], distance - 1, *chunks[c])
        return total

    marks[mid] = (tokens[0] + 1).astype(F32).astype(BF)
    zero_ends(marks)
    zero_ends(pre_grads)
    barrier = pltpu.get_barrier_semaphore()
    partners = [sibling, across] + [along(d) for d in range(1, ctx_count)]
    for partner in partners:
        pl.semaphore_signal(barrier, inc=1, device_id=partner, device_id_type=MESH)
    pl.semaphore_wait(barrier, len(partners))
    halo_start(marks, 0)

    flip_c = exchange(half_c)
    flip_h = exchange(half_h)
    stem_both = jnp.concatenate([stem[...], mm(stem[...], flip_c).astype(BF)], axis=1)
    for k in range(taps):
        conv_low[k] = mm(flip_c, conv[k, half_c:]).astype(BF)
    point_high = point[0:half_h]
    point_low = mm(flip_h, point[half_h:]).astype(BF)
    point_a = jnp.concatenate([point_high, point_low], axis=1)
    point_b = jnp.concatenate([point_low, point_high], axis=1)

    def embed_part(start, size):
        part = slice(start, start + size)
        hot, hot_rev = onehots(marks[part])
        ordered, reverse, inv, one, other = embed_rows(hot, hot_rev, stem_both, half_c)
        normed[part] = one
        normed_rev[part] = other
        return hot, hot_rev, ordered, reverse, inv

    hot, hot_rev, ordered, reverse, inv = embed_part(width, rows)
    embed = jnp.concatenate([ordered[:, :half_c], reverse[:, :half_c]], axis=1).astype(F32)
    halo_wait(marks, 0)
    embed_part(0, width)
    embed_part(width + rows, width)

    def tap(ref, k):
        return ref[k * step : k * step + rows]

    pre_a = sum(mm(tap(normed, k), conv[k]) for k in range(taps))
    pre_b = sum(mm(tap(normed_rev, k), conv[taps - 1 - k]) for k in range(taps))
    pre = jnp.concatenate([pre_a, pre_b], axis=1)
    cdf = normal_cdf(pre)
    act = (pre * cdf).astype(BF)
    slope = cdf + pre * normal_pdf(pre)
    act_a, act_b = act[:, :half_h], act[:, half_h:]
    after = (embed + mm(act_a, point_a) + mm(act_b, point_b)).astype(BF)
    head_both = jnp.concatenate([head[...], head[...]], axis=0)
    logits = mm(after, head_both)
    loss_grad = ((jnp.exp(logits) - targets[0].astype(F32)) * scale).astype(BF)
    up = mm_nt(loss_grad, head[...]).astype(BF)
    blocks = ctx_count * dp_count
    head_rows, point_rows = o_head.shape[0], o_point.shape[0]
    g_head = mm_tn(
        jnp.concatenate([loss_grad, loss_grad], axis=0),
        jnp.concatenate([after[:, :half_c], after[:, half_c:]], axis=0),
    )
    for n in range(blocks):
        grad[0][n // 2, n % 2, 0:head_rows] = g_head[n * head_rows : (n + 1) * head_rows]
    act_all = jnp.concatenate(
        [
            jnp.concatenate([act_a, mm(act_b, flip_h).astype(BF)], axis=1),
            jnp.concatenate([act_b, mm(act_a, flip_h).astype(BF)], axis=1),
        ],
        axis=0,
    )
    g_point = mm_tn(act_all, jnp.concatenate([up, up], axis=0))
    for n in range(blocks):
        grad[0][n // 2, n % 2, head_rows : head_rows + point_rows] = g_point[
            n * point_rows : (n + 1) * point_rows
        ]
    core_copy(0).start()

    up_both = jnp.concatenate([up, up], axis=1)
    act_grad = mm_nt(up_both, point_a)
    pre_grad = (jnp.concatenate([act_grad, act_grad], axis=1) * slope).astype(BF)
    pre_grads[mid] = pre_grad
    halo_start(pre_grads, 1)

    conv_rows = o_conv.shape[0]
    conv_cols = chunks[1][1]
    grads = jnp.concatenate([pre_grad[:, :half_h], pre_grad[:, half_h:]], axis=0)
    for k in range(taps):
        if k == 2:
            x_stage(0)
        both = jnp.concatenate([tap(normed, k), tap(normed_rev, taps - 1 - k)], axis=0)
        term = mm_tn(both, grads)
        first, end = k * 2 * half_c, (k + 1) * 2 * half_c
        at = first
        while at < end:
            n = at // conv_rows
            stop = min(end, (n + 1) * conv_rows)
            for c in range(half_h // conv_cols):
                grad[1 + c][n // 2, n % 2, at - n * conv_rows : stop - n * conv_rows] = term[
                    at - first : stop - first, c * conv_cols : (c + 1) * conv_cols
                ]
            at = stop
    core_copy(1).start()
    core_copy(2).start()
    for distance in range(1, ctx_count - 1):
        z_part(0, distance)
    x_stage(1)

    halo_wait(pre_grads, 1)
    normed_grad = jnp.zeros((rows, 2 * half_c), F32)
    for k in range(taps):
        weight = jnp.concatenate(
            [
                jnp.concatenate([conv[k, 0:half_c], conv_low[taps - 1 - k]], axis=1),
                jnp.concatenate([conv_low[k], conv[taps - 1 - k, 0:half_c]], axis=1),
            ],
            axis=0,
        )
        normed_grad = normed_grad + mm_nt(tap(pre_grads, taps - 1 - k), weight)
    inner = jnp.mean(normed_grad * embed, axis=1, keepdims=True)
    embed_grad = (
        inv * normed_grad - embed * inv * inv * inv * inner + up_both.astype(F32)
    ).astype(BF)
    g_stem = mm_tn(
        jnp.concatenate([hot, hot_rev], axis=0),
        jnp.concatenate([embed_grad[:, :half_c], embed_grad[:, half_c:]], axis=0),
    )
    stem_rows = o_stem.shape[0]
    for n in range(blocks):
        grad[3][n // 2, n % 2] = g_stem[n * stem_rows : (n + 1) * stem_rows]
    core_copy(3).start()

    z_part(0, ctx_count - 1)
    x_stage(2)
    z_stage(1)
    x_stage(3)
    z_stage(2)
    z_stage(3)
    total = last_stage(0)
    o_head[...] = total[0:head_rows]
    o_point[...] = total[head_rows : head_rows + point_rows]
    o_conv[:, 0:conv_cols] = last_stage(1)
    o_conv[:, conv_cols : 2 * conv_cols] = last_stage(2)
    o_stem[...] = last_stage(3)

    halo_sent(marks, 0)
    halo_sent(pre_grads, 1)
    for c in range(count):
        core_copy(c).wait_send()
        for slot in range(ctx_count):
            x_copy(c, slot).wait_send()
        for distance in range(1, ctx_count):
            z_copy(c, distance).wait_send()


def hand_out(*refs):
    copies = [pltpu.make_async_copy(refs[i], refs[4 + i], refs[8].at[i]) for i in range(4)]
    for copy in copies:
        copy.start()
    for copy in copies:
        copy.wait()


def local(tokens, targets, stem, conv, point, head):
    ctx_count = lax.axis_size("ctx")
    dp_count = lax.axis_size("dp")
    rows = tokens.shape[1]
    taps = conv.shape[0]
    half_c, half_h = stem.shape[1], conv.shape[2]
    width = (taps // 2) * DILATION_STEP
    blocks = ctx_count * dp_count
    totals = (stem.shape[0], taps * 2 * half_c, point.shape[0], head.shape[1])
    fits = all(total % (8 * blocks) == 0 for total in totals)
    if not (fits and dp_count == 4 and 2 <= ctx_count <= 4 and rows >= width and tokens.shape[0] == 1):
        return plain(tokens, targets, stem, conv, point, head)
    out_rows = [total // blocks for total in totals]
    chunks = (
        (out_rows[3] + out_rows[2], half_c),
        (out_rows[1], half_h // 2),
        (out_rows[1], half_h // 2),
        (out_rows[0], half_c),
    )
    vmem = pl.BlockSpec(memory_space=pltpu.VMEM)
    scratch = [
        pltpu.VMEM((rows + 2 * width, tokens.shape[2]), BF),
        pltpu.VMEM((rows + 2 * width, 2 * half_h), BF),
        pltpu.VMEM((rows + 2 * width, 2 * half_c), BF),
        pltpu.VMEM((rows + 2 * width, 2 * half_c), BF),
        pltpu.VMEM((taps, half_c, half_h), BF),
    ]
    scratch += [pltpu.VMEM((blocks // 2, 2, r, c), F32) for r, c in chunks]
    scratch += [pltpu.VMEM((blocks // 2, r, c), F32) for r, c in chunks]
    for slots in (ctx_count, ctx_count, ctx_count - 1, ctx_count - 1):
        scratch += [pltpu.VMEM((slots, packed_rows(r, c), 128), jnp.int16) for r, c in chunks]
    dma = pltpu.SemaphoreType.DMA
    count = len(chunks)
    scratch += [dma((4,)), dma((4,))]
    scratch += [dma((count,)), dma((count,))]
    scratch += [dma((count * ctx_count,)) for _ in range(2)]
    scratch += [dma((count * (ctx_count - 1),)) for _ in range(2)]
    sums = pl.pallas_call(
        functools.partial(kernel, ctx_count, dp_count, chunks),
        out_shape=(
            jax.ShapeDtypeStruct((out_rows[0], half_c), F32),
            jax.ShapeDtypeStruct((out_rows[1], half_h), F32),
            jax.ShapeDtypeStruct((out_rows[2], half_c), F32),
            jax.ShapeDtypeStruct((out_rows[3], half_c), F32),
        ),
        in_specs=[vmem] * 6,
        out_specs=(vmem,) * 4,
        scratch_shapes=scratch,
        compiler_params=pltpu.CompilerParams(
            collective_id=0, has_side_effects=True, vmem_limit_bytes=56 * 1024 * 1024
        ),
        name="step",
    )(tokens, targets, stem, conv, point, head)
    anywhere = pl.BlockSpec(memory_space=pl.ANY)
    return pl.pallas_call(
        hand_out,
        out_shape=tuple(jax.ShapeDtypeStruct(x.shape, x.dtype) for x in sums),
        in_specs=[anywhere] * 4,
        out_specs=(anywhere,) * 4,
        scratch_shapes=[dma((4,))],
        name="hand_out",
    )(*sums)


def solution(mesh):
    return jax.shard_map(
        local,
        mesh=mesh,
        in_specs=(
            P(("groups", "dp"), "ctx", None),
            P(("groups", "dp"), "ctx", None),
            P("groups", None),
            P("groups", None, None),
            P("groups", None),
            P("groups", None),
        ),
        out_specs=(P(("groups", "ctx", "dp"), None),) * 4,
        check_vma=False,
    )
```

```python
import functools
import math

import jax
import jax.numpy as jnp
from jax import lax
from jax.experimental import pallas as pl
from jax.experimental.pallas import tpu as pltpu
from jax.sharding import PartitionSpec as P

DILATION_STEP = 128
BF = jnp.bfloat16
F32 = jnp.float32


def mm(a, b):
    return lax.dot_general(a, b, (((1,), (0,)), ((), ())), preferred_element_type=F32)


def mm_nt(a, b):
    return lax.dot_general(a, b, (((1,), (1,)), ((), ())), preferred_element_type=F32)


def mm_tn(a, b):
    return lax.dot_general(a, b, (((0,), (0,)), ((), ())), preferred_element_type=F32)


def exchange(size):
    row = lax.broadcasted_iota(jnp.int32, (size, size), 0)
    col = lax.broadcasted_iota(jnp.int32, (size, size), 1)
    return jnp.where(row + col == size - 1, 1.0, 0.0).astype(BF)


def onehots(marks):
    bases = marks.shape[1]
    row = lax.broadcasted_iota(jnp.int32, (bases, 4 * bases), 0)
    col = lax.broadcasted_iota(jnp.int32, (bases, 4 * bases), 1)
    spread = jnp.where(row == lax.shift_right_logical(col, 2), 1.0, 0.0).astype(BF)
    spread_rev = jnp.where(bases - 1 - row == lax.shift_right_logical(col, 2), 1.0, 0.0).astype(BF)
    base = jnp.bitwise_and(lax.broadcasted_iota(jnp.int32, (1, 4 * bases), 1), 3).astype(F32)
    hot = jnp.where(mm(marks, spread) == base + 1.0, 1.0, 0.0).astype(BF)
    hot_rev = jnp.where(mm(marks, spread_rev) == 4.0 - base, 1.0, 0.0).astype(BF)
    return hot, hot_rev


def embed_rows(hot, hot_rev, stem_both, half_c):
    plain = mm(hot, stem_both).astype(BF)
    other = mm(hot_rev, stem_both).astype(BF)
    ordered = jnp.concatenate([plain[:, :half_c], other[:, half_c:]], axis=1)
    reverse = jnp.concatenate([other[:, :half_c], plain[:, half_c:]], axis=1)
    wide = ordered.astype(F32)
    inv_root = lax.rsqrt(jnp.mean(wide * wide, axis=1, keepdims=True) + 1e-05)
    normed = (wide * inv_root).astype(BF)
    normed_rev = (reverse.astype(F32) * inv_root).astype(BF)
    return ordered, reverse, inv_root, normed, normed_rev


def normal_cdf(values):
    return 0.5 * (1.0 + lax.erf(values * (1.0 / math.sqrt(2.0))))


def normal_pdf(values):
    return jnp.exp(-0.5 * values * values) * (1.0 / math.sqrt(2.0 * math.pi))


def halo(x, width):
    count = lax.axis_size("ctx")
    up = [(i, i + 1) for i in range(count - 1)]
    down = [(j, i) for i, j in up]
    before = lax.ppermute(x[x.shape[0] - width :], "ctx", up)
    after = lax.ppermute(x[:width], "ctx", down)
    return jnp.concatenate([before, x, after], axis=0)


def plain(tokens, targets, stem, conv, point, head):
    ctx_count = lax.axis_size("ctx")
    dp_count = lax.axis_size("dp")
    rows = tokens.shape[1]
    taps = conv.shape[0]
    half_c, half_h = stem.shape[1], conv.shape[2]
    width = (taps // 2) * DILATION_STEP
    step = DILATION_STEP
    scale = 1.0 / math.sqrt(rows * ctx_count * dp_count)

    marks = halo((tokens[0] + 1).astype(BF), width)
    flip_c = exchange(half_c)
    flip_h = exchange(half_h)
    stem_both = jnp.concatenate([stem, mm(stem, flip_c).astype(BF)], axis=1)
    conv_low = [mm(flip_c, conv[k, half_c:]).astype(BF) for k in range(taps)]
    point_low = mm(flip_h, point[half_h:]).astype(BF)
    point_a = jnp.concatenate([point[:half_h], point_low], axis=1)
    point_b = jnp.concatenate([point_low, point[:half_h]], axis=1)
    head_both = jnp.concatenate([head, head], axis=0)

    hot, hot_rev = onehots(marks)
    ordered, reverse, inv_root, normed, normed_rev = embed_rows(hot, hot_rev, stem_both, half_c)
    mid = slice(width, width + rows)
    inv = inv_root[mid]
    embed = jnp.concatenate([ordered[mid, :half_c], reverse[mid, :half_c]], axis=1).astype(F32)

    def tap(x, k):
        return x[k * step : k * step + rows]

    pre_a = sum(mm(tap(normed, k), conv[k]) for k in range(taps))
    pre_b = sum(mm(tap(normed_rev, k), conv[taps - 1 - k]) for k in range(taps))
    pre = jnp.concatenate([pre_a, pre_b], axis=1)
    cdf = normal_cdf(pre)
    act = (pre * cdf).astype(BF)
    act_a, act_b = act[:, :half_h], act[:, half_h:]
    after = (embed + mm(act_a, point_a) + mm(act_b, point_b)).astype(BF)
    logits = mm(after, head_both)
    loss_grad = ((jnp.exp(logits) - targets[0].astype(F32)) * scale).astype(BF)
    up = mm_nt(loss_grad, head).astype(BF)
    up_both = jnp.concatenate([up, up], axis=1)
    act_grad = mm_nt(up_both, point_a)
    slope = cdf + pre * normal_pdf(pre)
    pre_grad = (jnp.concatenate([act_grad, act_grad], axis=1) * slope).astype(BF)
    pre_halo = halo(pre_grad, width)

    g_head = mm_tn(
        jnp.concatenate([loss_grad, loss_grad], axis=0),
        jnp.concatenate([after[:, :half_c], after[:, half_c:]], axis=0),
    )
    act_all = jnp.concatenate(
        [
            jnp.concatenate([act_a, mm(act_b, flip_h).astype(BF)], axis=1),
            jnp.concatenate([act_b, mm(act_a, flip_h).astype(BF)], axis=1),
        ],
        axis=0,
    )
    g_point = mm_tn(act_all, jnp.concatenate([up, up], axis=0))
    grads = jnp.concatenate([pre_grad[:, :half_h], pre_grad[:, half_h:]], axis=0)
    g_conv = jnp.concatenate(
        [
            mm_tn(jnp.concatenate([tap(normed, k), tap(normed_rev, taps - 1 - k)], axis=0), grads)
            for k in range(taps)
        ],
        axis=0,
    )
    normed_grad = jnp.zeros((rows, 2 * half_c), F32)
    for k in range(taps):
        piece = tap(pre_halo, taps - 1 - k)
        weight = jnp.concatenate(
            [
                jnp.concatenate([conv[k, :half_c], conv_low[taps - 1 - k]], axis=1),
                jnp.concatenate([conv_low[k], conv[taps - 1 - k, :half_c]], axis=1),
            ],
            axis=0,
        )
        normed_grad = normed_grad + mm_nt(piece, weight)
    inner = jnp.mean(normed_grad * embed, axis=1, keepdims=True)
    embed_grad = (
        inv * normed_grad - embed * inv * inv * inv * inner + up_both.astype(F32)
    ).astype(BF)
    g_stem = mm_tn(
        jnp.concatenate([hot[mid], hot_rev[mid]], axis=0),
        jnp.concatenate([embed_grad[:, :half_c], embed_grad[:, half_c:]], axis=0),
    )

    def reduce(term):
        blocks = term.reshape(ctx_count, dp_count, -1, term.shape[1])
        by_dp = lax.psum_scatter(jnp.swapaxes(blocks, 0, 1), "dp", scatter_dimension=0)
        return lax.psum_scatter(by_dp, "ctx", scatter_dimension=0)

    return reduce(g_stem), reduce(g_conv), reduce(g_point), reduce(g_head)

MESH = pl.DeviceIdType.MESH


def packed_rows(rows, cols):
    return -(-(cols // 128 * rows + 8) // 16) * 16


def encode(values, out, slot):
    rows, cols = values.shape
    groups = cols // 128
    tail = packed_rows(rows, cols) - groups * rows
    largest = jnp.maximum(jnp.max(jnp.abs(values), axis=0, keepdims=True), 1e-30)
    power = jnp.ceil(jnp.log2(largest))
    scaled = jnp.clip(jnp.round(values * jnp.exp2(15.0 - power)), -32767.0, 32767.0)
    line = lax.broadcasted_iota(jnp.int32, (tail, 128), 0)
    last = jnp.zeros((tail, 128), F32)
    pieces = []
    for g in range(groups):
        lanes = slice(g * 128, (g + 1) * 128)
        pieces.append(scaled[:, lanes])
        last = jnp.where(line == g, power[:, lanes], last)
    out[slot] = jnp.concatenate(pieces + [last], axis=0).astype(jnp.int32).astype(jnp.int16)


def decode(ref, slot, rows, cols):
    values = ref[slot].astype(jnp.int32).astype(F32)
    groups = cols // 128
    last = groups * rows
    pieces = []
    for g in range(groups):
        power = values[last + g : last + g + 1]
        pieces.append(values[g * rows : (g + 1) * rows] * jnp.exp2(power - 15.0))
    return pieces[0] if groups == 1 else jnp.concatenate(pieces, axis=1)


def kernel(ctx_count, dp_count, chunks, *refs):
    in_sems, out_sems = refs[-2:]
    tokens, targets, stem, conv, point, head = refs[-12:-6]
    o_stem, o_conv, o_point, o_head = refs[-6:-2]
    loads = [pltpu.make_async_copy(refs[i], refs[i - 12], in_sems.at[i]) for i in range(6)]
    stores = [pltpu.make_async_copy(refs[i - 6], refs[i + 6], out_sems.at[i]) for i in range(4)]
    refs = refs[:-12]
    marks, pre_grads, normed, normed_rev, conv_low = refs[10:15]
    count = len(chunks)
    grad = refs[15 : 15 + count]
    from_core = refs[15 + count : 15 + 2 * count]
    to_x = refs[15 + 2 * count : 15 + 3 * count]
    from_x = refs[15 + 3 * count : 15 + 4 * count]
    to_z = refs[15 + 4 * count : 15 + 5 * count]
    from_z = refs[15 + 5 * count : 15 + 6 * count]
    (halo_send, halo_recv, core_send, core_recv, x_send, x_recv, z_send, z_recv) = refs[15 + 6 * count :]

    group = lax.axis_index("groups")
    ctx = lax.axis_index("ctx")
    dp = lax.axis_index("dp")
    core = lax.rem(dp, 2)
    side = dp // 2
    sibling = (group, ctx, dp + 1 - 2 * core)
    across = (group, ctx, lax.rem(dp + 2, dp_count))

    def along(distance):
        return (group, lax.rem(ctx + distance, ctx_count), dp)

    rows = tokens.shape[1]
    taps = conv.shape[0]
    half_c, half_h = stem.shape[1], conv.shape[2]
    width = (taps // 2) * DILATION_STEP
    step = DILATION_STEP
    mid = slice(width, width + rows)
    scale = 1.0 / math.sqrt(rows * ctx_count * dp_count)

    def zero_ends(buffer):
        zeros = jnp.zeros((width, buffer.shape[1]), buffer.dtype)

        @pl.when(ctx == 0)
        def _():
            buffer[0:width] = zeros

        @pl.when(ctx == ctx_count - 1)
        def _():
            buffer[width + rows : 2 * width + rows] = zeros

    def halo_copies(buffer, kind):
        upward = pltpu.make_async_remote_copy(
            src_ref=buffer.at[rows : rows + width],
            dst_ref=buffer.at[0:width],
            send_sem=halo_send.at[2 * kind],
            recv_sem=halo_recv.at[2 * kind],
            device_id=along(1),
            device_id_type=MESH,
        )
        downward = pltpu.make_async_remote_copy(
            src_ref=buffer.at[width : 2 * width],
            dst_ref=buffer.at[width + rows : 2 * width + rows],
            send_sem=halo_send.at[2 * kind + 1],
            recv_sem=halo_recv.at[2 * kind + 1],
            device_id=along(ctx_count - 1),
            device_id_type=MESH,
        )
        return upward, downward

    def halo_start(buffer, kind):
        upward, downward = halo_copies(buffer, kind)
        pl.when(ctx < ctx_count - 1)(upward.start)
        pl.when(ctx > 0)(downward.start)

    def halo_wait(buffer, kind):
        upward, downward = halo_copies(buffer, kind)
        pl.when(ctx > 0)(upward.wait_recv)
        pl.when(ctx < ctx_count - 1)(downward.wait_recv)

    def halo_sent(buffer, kind):
        upward, downward = halo_copies(buffer, kind)
        pl.when(ctx < ctx_count - 1)(upward.wait_send)
        pl.when(ctx > 0)(downward.wait_send)

    def core_copy(c):
        return pltpu.make_async_remote_copy(
            src_ref=grad[c].at[:, 1 - core],
            dst_ref=from_core[c],
            send_sem=core_send.at[c],
            recv_sem=core_recv.at[c],
            device_id=sibling,
            device_id_type=MESH,
        )

    def x_copy(c, slot):
        return pltpu.make_async_remote_copy(
            src_ref=to_x[c].at[slot],
            dst_ref=from_x[c].at[slot],
            send_sem=x_send.at[c * ctx_count + slot],
            recv_sem=x_recv.at[c * ctx_count + slot],
            device_id=across,
            device_id_type=MESH,
        )

    def z_copy(c, distance):
        return pltpu.make_async_remote_copy(
            src_ref=to_z[c].at[distance - 1],
            dst_ref=from_z[c].at[distance - 1],
            send_sem=z_send.at[c * (ctx_count - 1) + distance - 1],
            recv_sem=z_recv.at[c * (ctx_count - 1) + distance - 1],
            device_id=along(distance),
            device_id_type=MESH,
        )

    def x_stage(c):
        core_copy(c).wait_recv()
        for slot in range(ctx_count):
            n = 2 * lax.rem(ctx + 1 + slot, ctx_count) + 1 - side
            encode(grad[c][n, core] + from_core[c][n], to_x[c], slot)
            x_copy(c, slot).start()

    def chip_sum(c, slot):
        x_copy(c, slot).wait_recv()
        n = 2 * lax.rem(ctx + 1 + slot, ctx_count) + side
        return grad[c][n, core] + from_core[c][n] + decode(from_x[c], slot, *chunks[c])

    def z_part(c, distance):
        encode(chip_sum(c, distance - 1), to_z[c], distance - 1)
        z_copy(c, distance).start()

    def z_stage(c):
        for distance in range(1, ctx_count):
            z_part(c, distance)

    def last_stage(c):
        total = chip_sum(c, ctx_count - 1)
        for distance in range(1, ctx_count):
            z_copy(c, distance).wait_recv()
            total = total + decode(from_z[c], distance - 1, *chunks[c])
        return total

    barrier = pltpu.get_barrier_semaphore()
    partners = [sibling, across] + [along(d) for d in range(1, ctx_count)]
    for partner in partners:
        pl.semaphore_signal(barrier, inc=1, device_id=partner, device_id_type=MESH)
    for i in (0, 2, 3, 4, 5, 1):
        loads[i].start()
    zero_ends(marks)
    zero_ends(pre_grads)
    loads[0].wait()
    marks[mid] = (tokens[0] + 1).astype(F32).astype(BF)
    pl.semaphore_wait(barrier, len(partners))
    halo_start(marks, 0)

    flip_c = exchange(half_c)
    flip_h = exchange(half_h)
    loads[2].wait()
    stem_both = jnp.concatenate([stem[...], mm(stem[...], flip_c).astype(BF)], axis=1)

    def embed_part(start, size):
        part = slice(start, start + size)
        hot, hot_rev = onehots(marks[part])
        ordered, reverse, inv, one, other = embed_rows(hot, hot_rev, stem_both, half_c)
        normed[part] = one
        normed_rev[part] = other
        return hot, hot_rev, ordered, reverse, inv

    hot, hot_rev, ordered, reverse, inv = embed_part(width, rows)
    embed = jnp.concatenate([ordered[:, :half_c], reverse[:, :half_c]], axis=1).astype(F32)
    loads[3].wait()
    for k in range(taps):
        conv_low[k] = mm(flip_c, conv[k, half_c:]).astype(BF)
    loads[4].wait()
    point_high = point[0:half_h]
    point_low = mm(flip_h, point[half_h:]).astype(BF)
    point_a = jnp.concatenate([point_high, point_low], axis=1)
    point_b = jnp.concatenate([point_low, point_high], axis=1)
    halo_wait(marks, 0)
    embed_part(0, width)
    embed_part(width + rows, width)

    def tap(ref, k):
        return ref[k * step : k * step + rows]

    pre_a = sum(mm(tap(normed, k), conv[k]) for k in range(taps))
    pre_b = sum(mm(tap(normed_rev, k), conv[taps - 1 - k]) for k in range(taps))
    pre = jnp.concatenate([pre_a, pre_b], axis=1)
    cdf = normal_cdf(pre)
    act = (pre * cdf).astype(BF)
    slope = cdf + pre * normal_pdf(pre)
    act_a, act_b = act[:, :half_h], act[:, half_h:]
    after = (embed + mm(act_a, point_a) + mm(act_b, point_b)).astype(BF)
    loads[5].wait()
    loads[1].wait()
    head_both = jnp.concatenate([head[...], head[...]], axis=0)
    logits = mm(after, head_both)
    loss_grad = ((jnp.exp(logits) - targets[0].astype(F32)) * scale).astype(BF)
    up = mm_nt(loss_grad, head[...]).astype(BF)
    blocks = ctx_count * dp_count
    head_rows, point_rows = o_head.shape[0], o_point.shape[0]
    g_head = mm_tn(
        jnp.concatenate([loss_grad, loss_grad], axis=0),
        jnp.concatenate([after[:, :half_c], after[:, half_c:]], axis=0),
    )
    for n in range(blocks):
        grad[0][n // 2, n % 2, 0:head_rows] = g_head[n * head_rows : (n + 1) * head_rows]
    act_all = jnp.concatenate(
        [
            jnp.concatenate([act_a, mm(act_b, flip_h).astype(BF)], axis=1),
            jnp.concatenate([act_b, mm(act_a, flip_h).astype(BF)], axis=1),
        ],
        axis=0,
    )
    g_point = mm_tn(act_all, jnp.concatenate([up, up], axis=0))
    for n in range(blocks):
        grad[0][n // 2, n % 2, head_rows : head_rows + point_rows] = g_point[
            n * point_rows : (n + 1) * point_rows
        ]
    core_copy(0).start()

    up_both = jnp.concatenate([up, up], axis=1)
    act_grad = mm_nt(up_both, point_a)
    pre_grad = (jnp.concatenate([act_grad, act_grad], axis=1) * slope).astype(BF)
    pre_grads[mid] = pre_grad
    halo_start(pre_grads, 1)

    conv_rows = o_conv.shape[0]
    conv_cols = chunks[1][1]
    grads = jnp.concatenate([pre_grad[:, :half_h], pre_grad[:, half_h:]], axis=0)
    for k in range(taps):
        if k == 2:
            x_stage(0)
        both = jnp.concatenate([tap(normed, k), tap(normed_rev, taps - 1 - k)], axis=0)
        term = mm_tn(both, grads)
        first, end = k * 2 * half_c, (k + 1) * 2 * half_c
        at = first
        while at < end:
            n = at // conv_rows
            stop = min(end, (n + 1) * conv_rows)
            for c in range(half_h // conv_cols):
                grad[1 + c][n // 2, n % 2, at - n * conv_rows : stop - n * conv_rows] = term[
                    at - first : stop - first, c * conv_cols : (c + 1) * conv_cols
                ]
            at = stop
    core_copy(1).start()
    core_copy(2).start()
    for distance in range(1, ctx_count - 1):
        z_part(0, distance)
    x_stage(1)

    halo_wait(pre_grads, 1)
    normed_grad = jnp.zeros((rows, 2 * half_c), F32)
    for k in range(taps):
        weight = jnp.concatenate(
            [
                jnp.concatenate([conv[k, 0:half_c], conv_low[taps - 1 - k]], axis=1),
                jnp.concatenate([conv_low[k], conv[taps - 1 - k, 0:half_c]], axis=1),
            ],
            axis=0,
        )
        normed_grad = normed_grad + mm_nt(tap(pre_grads, taps - 1 - k), weight)
    inner = jnp.mean(normed_grad * embed, axis=1, keepdims=True)
    embed_grad = (
        inv * normed_grad - embed * inv * inv * inv * inner + up_both.astype(F32)
    ).astype(BF)
    g_stem = mm_tn(
        jnp.concatenate([hot, hot_rev], axis=0),
        jnp.concatenate([embed_grad[:, :half_c], embed_grad[:, half_c:]], axis=0),
    )
    stem_rows = o_stem.shape[0]
    for n in range(blocks):
        grad[3][n // 2, n % 2] = g_stem[n * stem_rows : (n + 1) * stem_rows]
    core_copy(3).start()

    z_part(0, ctx_count - 1)
    x_stage(2)
    z_stage(1)
    x_stage(3)
    z_stage(2)
    z_stage(3)
    total = last_stage(0)
    o_head[...] = total[0:head_rows]
    o_point[...] = total[head_rows : head_rows + point_rows]
    stores[3].start()
    stores[2].start()
    o_conv[:, 0:conv_cols] = last_stage(1)
    o_conv[:, conv_cols : 2 * conv_cols] = last_stage(2)
    stores[1].start()
    o_stem[...] = last_stage(3)
    stores[0].start()

    halo_sent(marks, 0)
    halo_sent(pre_grads, 1)
    for store in stores:
        store.wait()
    for c in range(count):
        core_copy(c).wait_send()
        for slot in range(ctx_count):
            x_copy(c, slot).wait_send()
        for distance in range(1, ctx_count):
            z_copy(c, distance).wait_send()


def hand_out(*refs):
    held, sems = refs[8:12], refs[12]
    arrive = [pltpu.make_async_copy(refs[i], held[i], sems.at[i]) for i in range(4)]
    leave = [pltpu.make_async_copy(held[i], refs[4 + i], sems.at[4 + i]) for i in range(4)]
    for copy in arrive:
        copy.start()
    for i in range(4):
        arrive[i].wait()
        leave[i].start()
    for copy in leave:
        copy.wait()


def local(tokens, targets, stem, conv, point, head):
    ctx_count = lax.axis_size("ctx")
    dp_count = lax.axis_size("dp")
    rows = tokens.shape[1]
    taps = conv.shape[0]
    half_c, half_h = stem.shape[1], conv.shape[2]
    width = (taps // 2) * DILATION_STEP
    blocks = ctx_count * dp_count
    totals = (stem.shape[0], taps * 2 * half_c, point.shape[0], head.shape[1])
    fits = all(total % (8 * blocks) == 0 for total in totals)
    if not (fits and dp_count == 4 and 2 <= ctx_count <= 4 and rows >= width and tokens.shape[0] == 1):
        return plain(tokens, targets, stem, conv, point, head)
    out_rows = [total // blocks for total in totals]
    chunks = (
        (out_rows[3] + out_rows[2], half_c),
        (out_rows[1], half_h // 2),
        (out_rows[1], half_h // 2),
        (out_rows[0], half_c),
    )
    arguments = (tokens, targets, stem, conv, point, head)
    anywhere = pl.BlockSpec(memory_space=pl.ANY)
    scratch = [
        pltpu.VMEM((rows + 2 * width, tokens.shape[2]), BF),
        pltpu.VMEM((rows + 2 * width, 2 * half_h), BF),
        pltpu.VMEM((rows + 2 * width, 2 * half_c), BF),
        pltpu.VMEM((rows + 2 * width, 2 * half_c), BF),
        pltpu.VMEM((taps, half_c, half_h), BF),
    ]
    scratch += [pltpu.VMEM((blocks // 2, 2, r, c), F32) for r, c in chunks]
    scratch += [pltpu.VMEM((blocks // 2, r, c), F32) for r, c in chunks]
    for slots in (ctx_count, ctx_count, ctx_count - 1, ctx_count - 1):
        scratch += [pltpu.VMEM((slots, packed_rows(r, c), 128), jnp.int16) for r, c in chunks]
    dma = pltpu.SemaphoreType.DMA
    count = len(chunks)
    scratch += [dma((4,)), dma((4,))]
    scratch += [dma((count,)), dma((count,))]
    scratch += [dma((count * ctx_count,)) for _ in range(2)]
    scratch += [dma((count * (ctx_count - 1),)) for _ in range(2)]
    outs = (
        jax.ShapeDtypeStruct((out_rows[0], half_c), F32),
        jax.ShapeDtypeStruct((out_rows[1], half_h), F32),
        jax.ShapeDtypeStruct((out_rows[2], half_c), F32),
        jax.ShapeDtypeStruct((out_rows[3], half_c), F32),
    )
    held = [pltpu.VMEM(x.shape, F32) for x in outs]
    scratch += [pltpu.VMEM(x.shape, x.dtype) for x in arguments] + held + [dma((6,)), dma((4,))]
    sums = pl.pallas_call(
        functools.partial(kernel, ctx_count, dp_count, chunks),
        out_shape=outs,
        in_specs=[anywhere] * 6,
        out_specs=(anywhere,) * 4,
        scratch_shapes=scratch,
        compiler_params=pltpu.CompilerParams(
            collective_id=0, has_side_effects=True, vmem_limit_bytes=56 * 1024 * 1024
        ),
        name="step",
    )(*arguments)
    return pl.pallas_call(
        hand_out,
        out_shape=outs,
        in_specs=[anywhere] * 4,
        out_specs=(anywhere,) * 4,
        scratch_shapes=held + [dma((8,))],
        name="hand_out",
    )(*sums)


def solution(mesh):
    return jax.shard_map(
        local,
        mesh=mesh,
        in_specs=(
            P(("groups", "dp"), "ctx", None),
            P(("groups", "dp"), "ctx", None),
            P("groups", None),
            P("groups", None, None),
            P("groups", None),
            P("groups", None),
        ),
        out_specs=(P(("groups", "ctx", "dp"), None),) * 4,
        check_vma=False,
    )
```

```python
import functools
import math

import jax
import jax.numpy as jnp
from jax import lax
from jax.experimental import pallas as pl
from jax.experimental.pallas import tpu as pltpu
from jax.sharding import PartitionSpec as P

DILATION_STEP = 128
BF = jnp.bfloat16
F32 = jnp.float32


def mm(a, b):
    return lax.dot_general(a, b, (((1,), (0,)), ((), ())), preferred_element_type=F32)


def mm_nt(a, b):
    return lax.dot_general(a, b, (((1,), (1,)), ((), ())), preferred_element_type=F32)


def mm_tn(a, b):
    return lax.dot_general(a, b, (((0,), (0,)), ((), ())), preferred_element_type=F32)


def exchange(size):
    row = lax.broadcasted_iota(jnp.int32, (size, size), 0)
    col = lax.broadcasted_iota(jnp.int32, (size, size), 1)
    return jnp.where(row + col == size - 1, 1.0, 0.0).astype(BF)


def onehots(marks):
    bases = marks.shape[1]
    row = lax.broadcasted_iota(jnp.int32, (bases, 4 * bases), 0)
    col = lax.broadcasted_iota(jnp.int32, (bases, 4 * bases), 1)
    spread = jnp.where(row == lax.shift_right_logical(col, 2), 1.0, 0.0).astype(BF)
    spread_rev = jnp.where(bases - 1 - row == lax.shift_right_logical(col, 2), 1.0, 0.0).astype(BF)
    base = jnp.bitwise_and(lax.broadcasted_iota(jnp.int32, (1, 4 * bases), 1), 3).astype(F32)
    hot = jnp.where(mm(marks, spread) == base + 1.0, 1.0, 0.0).astype(BF)
    hot_rev = jnp.where(mm(marks, spread_rev) == 4.0 - base, 1.0, 0.0).astype(BF)
    return hot, hot_rev


def embed_rows(hot, hot_rev, stem_both, half_c):
    plain = mm(hot, stem_both).astype(BF)
    other = mm(hot_rev, stem_both).astype(BF)
    ordered = jnp.concatenate([plain[:, :half_c], other[:, half_c:]], axis=1)
    reverse = jnp.concatenate([other[:, :half_c], plain[:, half_c:]], axis=1)
    wide = ordered.astype(F32)
    inv_root = lax.rsqrt(jnp.mean(wide * wide, axis=1, keepdims=True) + 1e-05)
    normed = (wide * inv_root).astype(BF)
    normed_rev = (reverse.astype(F32) * inv_root).astype(BF)
    return ordered, reverse, inv_root, normed, normed_rev


def normal_cdf(values):
    return 0.5 * (1.0 + lax.erf(values * (1.0 / math.sqrt(2.0))))


def normal_pdf(values):
    return jnp.exp(-0.5 * values * values) * (1.0 / math.sqrt(2.0 * math.pi))


def halo(x, width):
    count = lax.axis_size("ctx")
    up = [(i, i + 1) for i in range(count - 1)]
    down = [(j, i) for i, j in up]
    before = lax.ppermute(x[x.shape[0] - width :], "ctx", up)
    after = lax.ppermute(x[:width], "ctx", down)
    return jnp.concatenate([before, x, after], axis=0)


def plain(tokens, targets, stem, conv, point, head):
    ctx_count = lax.axis_size("ctx")
    dp_count = lax.axis_size("dp")
    rows = tokens.shape[1]
    taps = conv.shape[0]
    half_c, half_h = stem.shape[1], conv.shape[2]
    width = (taps // 2) * DILATION_STEP
    step = DILATION_STEP
    scale = 1.0 / math.sqrt(rows * ctx_count * dp_count)

    marks = halo((tokens[0] + 1).astype(BF), width)
    flip_c = exchange(half_c)
    flip_h = exchange(half_h)
    stem_both = jnp.concatenate([stem, mm(stem, flip_c).astype(BF)], axis=1)
    conv_low = [mm(flip_c, conv[k, half_c:]).astype(BF) for k in range(taps)]
    point_low = mm(flip_h, point[half_h:]).astype(BF)
    point_a = jnp.concatenate([point[:half_h], point_low], axis=1)
    point_b = jnp.concatenate([point_low, point[:half_h]], axis=1)
    head_both = jnp.concatenate([head, head], axis=0)

    hot, hot_rev = onehots(marks)
    ordered, reverse, inv_root, normed, normed_rev = embed_rows(hot, hot_rev, stem_both, half_c)
    mid = slice(width, width + rows)
    inv = inv_root[mid]
    embed = jnp.concatenate([ordered[mid, :half_c], reverse[mid, :half_c]], axis=1).astype(F32)

    def tap(x, k):
        return x[k * step : k * step + rows]

    pre_a = sum(mm(tap(normed, k), conv[k]) for k in range(taps))
    pre_b = sum(mm(tap(normed_rev, k), conv[taps - 1 - k]) for k in range(taps))
    pre = jnp.concatenate([pre_a, pre_b], axis=1)
    cdf = normal_cdf(pre)
    act = (pre * cdf).astype(BF)
    act_a, act_b = act[:, :half_h], act[:, half_h:]
    after = (embed + mm(act_a, point_a) + mm(act_b, point_b)).astype(BF)
    logits = mm(after, head_both)
    loss_grad = ((jnp.exp(logits) - targets[0].astype(F32)) * scale).astype(BF)
    up = mm_nt(loss_grad, head).astype(BF)
    up_both = jnp.concatenate([up, up], axis=1)
    act_grad = mm_nt(up_both, point_a)
    slope = cdf + pre * normal_pdf(pre)
    pre_grad = (jnp.concatenate([act_grad, act_grad], axis=1) * slope).astype(BF)
    pre_halo = halo(pre_grad, width)

    g_head = mm_tn(
        jnp.concatenate([loss_grad, loss_grad], axis=0),
        jnp.concatenate([after[:, :half_c], after[:, half_c:]], axis=0),
    )
    act_all = jnp.concatenate(
        [
            jnp.concatenate([act_a, mm(act_b, flip_h).astype(BF)], axis=1),
            jnp.concatenate([act_b, mm(act_a, flip_h).astype(BF)], axis=1),
        ],
        axis=0,
    )
    g_point = mm_tn(act_all, jnp.concatenate([up, up], axis=0))
    grads = jnp.concatenate([pre_grad[:, :half_h], pre_grad[:, half_h:]], axis=0)
    g_conv = jnp.concatenate(
        [
            mm_tn(jnp.concatenate([tap(normed, k), tap(normed_rev, taps - 1 - k)], axis=0), grads)
            for k in range(taps)
        ],
        axis=0,
    )
    normed_grad = jnp.zeros((rows, 2 * half_c), F32)
    for k in range(taps):
        piece = tap(pre_halo, taps - 1 - k)
        weight = jnp.concatenate(
            [
                jnp.concatenate([conv[k, :half_c], conv_low[taps - 1 - k]], axis=1),
                jnp.concatenate([conv_low[k], conv[taps - 1 - k, :half_c]], axis=1),
            ],
            axis=0,
        )
        normed_grad = normed_grad + mm_nt(piece, weight)
    inner = jnp.mean(normed_grad * embed, axis=1, keepdims=True)
    embed_grad = (
        inv * normed_grad - embed * inv * inv * inv * inner + up_both.astype(F32)
    ).astype(BF)
    g_stem = mm_tn(
        jnp.concatenate([hot[mid], hot_rev[mid]], axis=0),
        jnp.concatenate([embed_grad[:, :half_c], embed_grad[:, half_c:]], axis=0),
    )

    def reduce(term):
        blocks = term.reshape(ctx_count, dp_count, -1, term.shape[1])
        by_dp = lax.psum_scatter(jnp.swapaxes(blocks, 0, 1), "dp", scatter_dimension=0)
        return lax.psum_scatter(by_dp, "ctx", scatter_dimension=0)

    return reduce(g_stem), reduce(g_conv), reduce(g_point), reduce(g_head)

MESH = pl.DeviceIdType.MESH


def packed_rows(rows, cols):
    return -(-(cols // 128 * rows + 8) // 16) * 16


def encode(values, out, slot):
    rows, cols = values.shape
    groups = cols // 128
    tail = packed_rows(rows, cols) - groups * rows
    largest = jnp.maximum(jnp.max(jnp.abs(values), axis=0, keepdims=True), 1e-30)
    power = jnp.ceil(jnp.log2(largest))
    scaled = jnp.clip(jnp.round(values * jnp.exp2(15.0 - power)), -32767.0, 32767.0)
    line = lax.broadcasted_iota(jnp.int32, (tail, 128), 0)
    last = jnp.zeros((tail, 128), F32)
    pieces = []
    for g in range(groups):
        lanes = slice(g * 128, (g + 1) * 128)
        pieces.append(scaled[:, lanes])
        last = jnp.where(line == g, power[:, lanes], last)
    out[slot] = jnp.concatenate(pieces + [last], axis=0).astype(jnp.int32).astype(jnp.int16)


def decode(ref, slot, rows, cols):
    values = ref[slot].astype(jnp.int32).astype(F32)
    groups = cols // 128
    last = groups * rows
    pieces = []
    for g in range(groups):
        power = values[last + g : last + g + 1]
        pieces.append(values[g * rows : (g + 1) * rows] * jnp.exp2(power - 15.0))
    return pieces[0] if groups == 1 else jnp.concatenate(pieces, axis=1)


def kernel(ctx_count, dp_count, chunks, *refs):
    in_sems, out_sems = refs[-2:]
    tokens, targets, stem, conv, point, head = refs[-12:-6]
    o_stem, o_conv, o_point, o_head = refs[-6:-2]
    loads = [pltpu.make_async_copy(refs[i], refs[i - 12], in_sems.at[i]) for i in range(6)]
    stores = [pltpu.make_async_copy(refs[i - 6], refs[i + 6], out_sems.at[i]) for i in range(4)]
    refs = refs[:-12]
    marks, pre_grads, normed, normed_rev, conv_low = refs[10:15]
    count = len(chunks)
    grad = refs[15 : 15 + count]
    from_core = refs[15 + count : 15 + 2 * count]
    to_x = refs[15 + 2 * count : 15 + 3 * count]
    from_x = refs[15 + 3 * count : 15 + 4 * count]
    to_z = refs[15 + 4 * count : 15 + 5 * count]
    from_z = refs[15 + 5 * count : 15 + 6 * count]
    (halo_send, halo_recv, core_send, core_recv, x_send, x_recv, z_send, z_recv) = refs[15 + 6 * count :]

    group = lax.axis_index("groups")
    ctx = lax.axis_index("ctx")
    dp = lax.axis_index("dp")
    core = lax.rem(dp, 2)
    side = dp // 2
    sibling = (group, ctx, dp + 1 - 2 * core)
    across = (group, ctx, lax.rem(dp + 2, dp_count))

    def along(distance):
        return (group, lax.rem(ctx + distance, ctx_count), dp)

    rows = tokens.shape[1]
    taps = conv.shape[0]
    half_c, half_h = stem.shape[1], conv.shape[2]
    width = (taps // 2) * DILATION_STEP
    step = DILATION_STEP
    mid = slice(width, width + rows)
    scale = 1.0 / math.sqrt(rows * ctx_count * dp_count)

    def zero_ends(buffer):
        zeros = jnp.zeros((width, buffer.shape[1]), buffer.dtype)

        @pl.when(ctx == 0)
        def _():
            buffer[0:width] = zeros

        @pl.when(ctx == ctx_count - 1)
        def _():
            buffer[width + rows : 2 * width + rows] = zeros

    def halo_copies(buffer, kind):
        upward = pltpu.make_async_remote_copy(
            src_ref=buffer.at[rows : rows + width],
            dst_ref=buffer.at[0:width],
            send_sem=halo_send.at[2 * kind],
            recv_sem=halo_recv.at[2 * kind],
            device_id=along(1),
            device_id_type=MESH,
        )
        downward = pltpu.make_async_remote_copy(
            src_ref=buffer.at[width : 2 * width],
            dst_ref=buffer.at[width + rows : 2 * width + rows],
            send_sem=halo_send.at[2 * kind + 1],
            recv_sem=halo_recv.at[2 * kind + 1],
            device_id=along(ctx_count - 1),
            device_id_type=MESH,
        )
        return upward, downward

    def halo_start(buffer, kind):
        upward, downward = halo_copies(buffer, kind)
        pl.when(ctx < ctx_count - 1)(upward.start)
        pl.when(ctx > 0)(downward.start)

    def halo_wait(buffer, kind):
        upward, downward = halo_copies(buffer, kind)
        pl.when(ctx > 0)(upward.wait_recv)
        pl.when(ctx < ctx_count - 1)(downward.wait_recv)

    def halo_sent(buffer, kind):
        upward, downward = halo_copies(buffer, kind)
        pl.when(ctx < ctx_count - 1)(upward.wait_send)
        pl.when(ctx > 0)(downward.wait_send)

    def core_copy(c):
        return pltpu.make_async_remote_copy(
            src_ref=grad[c].at[:, 1 - core],
            dst_ref=from_core[c],
            send_sem=core_send.at[c],
            recv_sem=core_recv.at[c],
            device_id=sibling,
            device_id_type=MESH,
        )

    def x_copy(c, slot):
        return pltpu.make_async_remote_copy(
            src_ref=to_x[c].at[slot],
            dst_ref=from_x[c].at[slot],
            send_sem=x_send.at[c * ctx_count + slot],
            recv_sem=x_recv.at[c * ctx_count + slot],
            device_id=across,
            device_id_type=MESH,
        )

    def z_copy(c, distance):
        return pltpu.make_async_remote_copy(
            src_ref=to_z[c].at[distance - 1],
            dst_ref=from_z[c].at[distance - 1],
            send_sem=z_send.at[c * (ctx_count - 1) + distance - 1],
            recv_sem=z_recv.at[c * (ctx_count - 1) + distance - 1],
            device_id=along(distance),
            device_id_type=MESH,
        )

    def x_stage(c):
        core_copy(c).wait_recv()
        for slot in range(ctx_count):
            n = 2 * lax.rem(ctx + 1 + slot, ctx_count) + 1 - side
            encode(grad[c][n, core] + from_core[c][n], to_x[c], slot)
            x_copy(c, slot).start()

    def chip_sum(c, slot):
        x_copy(c, slot).wait_recv()
        n = 2 * lax.rem(ctx + 1 + slot, ctx_count) + side
        return grad[c][n, core] + from_core[c][n] + decode(from_x[c], slot, *chunks[c])

    def z_part(c, distance):
        encode(chip_sum(c, distance - 1), to_z[c], distance - 1)
        z_copy(c, distance).start()

    def z_stage(c):
        for distance in range(1, ctx_count):
            z_part(c, distance)

    def last_stage(c):
        total = chip_sum(c, ctx_count - 1)
        for distance in range(1, ctx_count):
            z_copy(c, distance).wait_recv()
            total = total + decode(from_z[c], distance - 1, *chunks[c])
        return total

    barrier = pltpu.get_barrier_semaphore()
    partners = [sibling, across] + [along(d) for d in range(1, ctx_count)]
    for partner in partners:
        pl.semaphore_signal(barrier, inc=1, device_id=partner, device_id_type=MESH)
    for i in (0, 2, 3, 4, 5, 1):
        loads[i].start()
    zero_ends(marks)
    zero_ends(pre_grads)
    loads[0].wait()
    marks[mid] = (tokens[0] + 1).astype(F32).astype(BF)
    pl.semaphore_wait(barrier, len(partners))
    halo_start(marks, 0)

    flip_c = exchange(half_c)
    flip_h = exchange(half_h)
    loads[2].wait()
    stem_both = jnp.concatenate([stem[...], mm(stem[...], flip_c).astype(BF)], axis=1)

    def embed_part(start, size):
        part = slice(start, start + size)
        hot, hot_rev = onehots(marks[part])
        ordered, reverse, inv, one, other = embed_rows(hot, hot_rev, stem_both, half_c)
        normed[part] = one
        normed_rev[part] = other
        return hot, hot_rev, ordered, reverse, inv

    hot, hot_rev, ordered, reverse, inv = embed_part(width, rows)
    embed = jnp.concatenate([ordered[:, :half_c], reverse[:, :half_c]], axis=1).astype(F32)
    loads[3].wait()
    for k in range(taps):
        conv_low[k] = mm(flip_c, conv[k, half_c:]).astype(BF)
    loads[4].wait()
    point_high = point[0:half_h]
    point_low = mm(flip_h, point[half_h:]).astype(BF)
    point_a = jnp.concatenate([point_high, point_low], axis=1)
    point_b = jnp.concatenate([point_low, point_high], axis=1)
    halo_wait(marks, 0)
    embed_part(0, width)
    embed_part(width + rows, width)

    def tap(ref, k):
        return ref[k * step : k * step + rows]

    pre_a = sum(mm(tap(normed, k), conv[k]) for k in range(taps))
    pre_b = sum(mm(tap(normed_rev, k), conv[taps - 1 - k]) for k in range(taps))
    pre = jnp.concatenate([pre_a, pre_b], axis=1)
    cdf = normal_cdf(pre)
    act = (pre * cdf).astype(BF)
    slope = cdf + pre * normal_pdf(pre)
    act_a, act_b = act[:, :half_h], act[:, half_h:]
    after = (embed + mm(act_a, point_a) + mm(act_b, point_b)).astype(BF)
    loads[5].wait()
    loads[1].wait()
    head_both = jnp.concatenate([head[...], head[...]], axis=0)
    logits = mm(after, head_both)
    loss_grad = ((jnp.exp(logits) - targets[0].astype(F32)) * scale).astype(BF)
    up = mm_nt(loss_grad, head[...]).astype(BF)
    blocks = ctx_count * dp_count
    head_rows, point_rows = o_head.shape[0], o_point.shape[0]
    g_head = mm_tn(
        jnp.concatenate([loss_grad, loss_grad], axis=0),
        jnp.concatenate([after[:, :half_c], after[:, half_c:]], axis=0),
    )
    for n in range(blocks):
        grad[0][n // 2, n % 2, 0:head_rows] = g_head[n * head_rows : (n + 1) * head_rows]
    act_all = jnp.concatenate(
        [
            jnp.concatenate([act_a, mm(act_b, flip_h).astype(BF)], axis=1),
            jnp.concatenate([act_b, mm(act_a, flip_h).astype(BF)], axis=1),
        ],
        axis=0,
    )
    g_point = mm_tn(act_all, jnp.concatenate([up, up], axis=0))
    for n in range(blocks):
        grad[0][n // 2, n % 2, head_rows : head_rows + point_rows] = g_point[
            n * point_rows : (n + 1) * point_rows
        ]
    core_copy(0).start()

    up_both = jnp.concatenate([up, up], axis=1)
    act_grad = mm_nt(up_both, point_a)
    pre_grad = (jnp.concatenate([act_grad, act_grad], axis=1) * slope).astype(BF)
    pre_grads[mid] = pre_grad
    halo_start(pre_grads, 1)

    conv_rows = o_conv.shape[0]
    conv_cols = chunks[1][1]
    grads = jnp.concatenate([pre_grad[:, :half_h], pre_grad[:, half_h:]], axis=0)
    for k in range(taps):
        if k == 2:
            x_stage(0)
        both = jnp.concatenate([tap(normed, k), tap(normed_rev, taps - 1 - k)], axis=0)
        term = mm_tn(both, grads)
        first, end = k * 2 * half_c, (k + 1) * 2 * half_c
        at = first
        while at < end:
            n = at // conv_rows
            stop = min(end, (n + 1) * conv_rows)
            for c in range(half_h // conv_cols):
                grad[1 + c][n // 2, n % 2, at - n * conv_rows : stop - n * conv_rows] = term[
                    at - first : stop - first, c * conv_cols : (c + 1) * conv_cols
                ]
            at = stop
    core_copy(1).start()
    core_copy(2).start()
    for distance in range(1, ctx_count - 1):
        z_part(0, distance)
    x_stage(1)
    z_part(0, ctx_count - 1)
    x_stage(2)

    halo_wait(pre_grads, 1)
    normed_grad = jnp.zeros((rows, 2 * half_c), F32)
    for k in range(taps):
        weight = jnp.concatenate(
            [
                jnp.concatenate([conv[k, 0:half_c], conv_low[taps - 1 - k]], axis=1),
                jnp.concatenate([conv_low[k], conv[taps - 1 - k, 0:half_c]], axis=1),
            ],
            axis=0,
        )
        normed_grad = normed_grad + mm_nt(tap(pre_grads, taps - 1 - k), weight)
    inner = jnp.mean(normed_grad * embed, axis=1, keepdims=True)
    embed_grad = (
        inv * normed_grad - embed * inv * inv * inv * inner + up_both.astype(F32)
    ).astype(BF)
    g_stem = mm_tn(
        jnp.concatenate([hot, hot_rev], axis=0),
        jnp.concatenate([embed_grad[:, :half_c], embed_grad[:, half_c:]], axis=0),
    )
    stem_rows = o_stem.shape[0]
    for n in range(blocks):
        grad[3][n // 2, n % 2] = g_stem[n * stem_rows : (n + 1) * stem_rows]
    core_copy(3).start()

    z_stage(1)
    x_stage(3)
    z_stage(2)
    z_stage(3)
    total = last_stage(0)
    o_head[...] = total[0:head_rows]
    o_point[...] = total[head_rows : head_rows + point_rows]
    stores[3].start()
    stores[2].start()
    o_conv[:, 0:conv_cols] = last_stage(1)
    o_conv[:, conv_cols : 2 * conv_cols] = last_stage(2)
    stores[1].start()
    o_stem[...] = last_stage(3)
    stores[0].start()

    halo_sent(marks, 0)
    halo_sent(pre_grads, 1)
    for store in stores:
        store.wait()
    for c in range(count):
        core_copy(c).wait_send()
        for slot in range(ctx_count):
            x_copy(c, slot).wait_send()
        for distance in range(1, ctx_count):
            z_copy(c, distance).wait_send()


def hand_out(*refs):
    held, sems = refs[8:12], refs[12]
    arrive = [pltpu.make_async_copy(refs[i], held[i], sems.at[i]) for i in range(4)]
    leave = [pltpu.make_async_copy(held[i], refs[4 + i], sems.at[4 + i]) for i in range(4)]
    for copy in arrive:
        copy.start()
    for i in range(4):
        arrive[i].wait()
        leave[i].start()
    for copy in leave:
        copy.wait()


def local(tokens, targets, stem, conv, point, head):
    ctx_count = lax.axis_size("ctx")
    dp_count = lax.axis_size("dp")
    rows = tokens.shape[1]
    taps = conv.shape[0]
    half_c, half_h = stem.shape[1], conv.shape[2]
    width = (taps // 2) * DILATION_STEP
    blocks = ctx_count * dp_count
    totals = (stem.shape[0], taps * 2 * half_c, point.shape[0], head.shape[1])
    fits = all(total % (8 * blocks) == 0 for total in totals)
    if not (fits and dp_count == 4 and 2 <= ctx_count <= 4 and rows >= width and tokens.shape[0] == 1):
        return plain(tokens, targets, stem, conv, point, head)
    out_rows = [total // blocks for total in totals]
    chunks = (
        (out_rows[3] + out_rows[2], half_c),
        (out_rows[1], half_h // 2),
        (out_rows[1], half_h // 2),
        (out_rows[0], half_c),
    )
    arguments = (tokens, targets, stem, conv, point, head)
    anywhere = pl.BlockSpec(memory_space=pl.ANY)
    scratch = [
        pltpu.VMEM((rows + 2 * width, tokens.shape[2]), BF),
        pltpu.VMEM((rows + 2 * width, 2 * half_h), BF),
        pltpu.VMEM((rows + 2 * width, 2 * half_c), BF),
        pltpu.VMEM((rows + 2 * width, 2 * half_c), BF),
        pltpu.VMEM((taps, half_c, half_h), BF),
    ]
    scratch += [pltpu.VMEM((blocks // 2, 2, r, c), F32) for r, c in chunks]
    scratch += [pltpu.VMEM((blocks // 2, r, c), F32) for r, c in chunks]
    for slots in (ctx_count, ctx_count, ctx_count - 1, ctx_count - 1):
        scratch += [pltpu.VMEM((slots, packed_rows(r, c), 128), jnp.int16) for r, c in chunks]
    dma = pltpu.SemaphoreType.DMA
    count = len(chunks)
    scratch += [dma((4,)), dma((4,))]
    scratch += [dma((count,)), dma((count,))]
    scratch += [dma((count * ctx_count,)) for _ in range(2)]
    scratch += [dma((count * (ctx_count - 1),)) for _ in range(2)]
    outs = (
        jax.ShapeDtypeStruct((out_rows[0], half_c), F32),
        jax.ShapeDtypeStruct((out_rows[1], half_h), F32),
        jax.ShapeDtypeStruct((out_rows[2], half_c), F32),
        jax.ShapeDtypeStruct((out_rows[3], half_c), F32),
    )
    held = [pltpu.VMEM(x.shape, F32) for x in outs]
    scratch += [pltpu.VMEM(x.shape, x.dtype) for x in arguments] + held + [dma((6,)), dma((4,))]
    sums = pl.pallas_call(
        functools.partial(kernel, ctx_count, dp_count, chunks),
        out_shape=outs,
        in_specs=[anywhere] * 6,
        out_specs=(anywhere,) * 4,
        scratch_shapes=scratch,
        compiler_params=pltpu.CompilerParams(
            collective_id=0, has_side_effects=True, vmem_limit_bytes=56 * 1024 * 1024
        ),
        name="step",
    )(*arguments)
    return pl.pallas_call(
        hand_out,
        out_shape=outs,
        in_specs=[anywhere] * 4,
        out_specs=(anywhere,) * 4,
        scratch_shapes=held + [dma((8,))],
        name="hand_out",
    )(*sums)


def solution(mesh):
    return jax.shard_map(
        local,
        mesh=mesh,
        in_specs=(
            P(("groups", "dp"), "ctx", None),
            P(("groups", "dp"), "ctx", None),
            P("groups", None),
            P("groups", None, None),
            P("groups", None),
            P("groups", None),
        ),
        out_specs=(P(("groups", "ctx", "dp"), None),) * 4,
        check_vma=False,
    )
```
